768 devices in a mesh: pipe: 192 (over z, y, core), tensor: 4 (over x).
Axes of the slice: x: 4, y: 8, z: 12, core: 2. Of those that a mesh axis runs over, the one named last changes fastest.
Arguments:
- query: bfloat16 [49152, 2048], P(('pipe', 'tensor')), may hold values from -20 to 20
- key: bfloat16 [49152, 1024], P(('pipe', 'tensor')), may hold values from -20 to 20
- value: bfloat16 [49152, 1024], P(('pipe', 'tensor')), may hold values from -6 to 6
- grad_out: bfloat16 [49152, 2048], P(('pipe', 'tensor')), may hold values from -6 to 6
- segment_ids: int32 [49152], replicated, may hold values from 0 to 47, never falling along the last dimension, each value on 1 to 2048 neighbouring positions
Outputs:
- attn_out: bfloat16 [49152, 2048], P(('pipe', 'tensor'))
- grad_query: bfloat16 [49152, 2048], P(('pipe', 'tensor'))
- grad_key: bfloat16 [49152, 1024], P(('pipe', 'tensor'))
- grad_value: bfloat16 [49152, 1024], P(('pipe', 'tensor'))
The draws below stay inside these ranges and needn't reach their ends.
Inputs may be any that keep to these rules, and one draw needn't show every extreme that they name: `segment_ids`: segment ids never fall along the tokens; each of the 48 documents holds 1 to 2048 tokens and one holds exactly 2048.
All inputs are finite; a program needn't handle non-finite values.
Results may differ from the reference program's by a relative error of at most 0.029.
Values may be sent and summed in bfloat16 or wider, within the bound.
A program may use at most 32 MiB of HBM per device.

```python
import math
import jax
import jax.numpy as jnp
import numpy as np
from jax import lax

Q_HEADS = 16
KV_HEADS = 8
HEAD_DIM = 128
WINDOW = 1024
TOK_DEV = 256
TOKENS = 49152
DOCS = 48
DOC_MOST = 2048


def base_rows(key, columns):
    return jnp.clip(jax.random.normal(key, (TOKENS, columns), jnp.float32), -4.0, 4.0)


def draw_query(key, part):
    base = base_rows(jax.random.fold_in(key, 21), Q_HEADS * HEAD_DIM)
    return base.astype(jnp.bfloat16)


def draw_key(key, part):
    base = base_rows(jax.random.fold_in(key, 33), KV_HEADS * HEAD_DIM)
    return base.astype(jnp.bfloat16)


def steps_of(rng, shape, split, smallest, top_value):
    level, own = 1.0, jax.random.fold_in(rng, 6)
    for axis_at, blocks in split:
        heights = jnp.exp(jax.random.uniform(jax.random.fold_in(own, axis_at), (blocks,), jnp.float32, smallest / len(split), top_value / len(split)))
        level = level * jnp.repeat(heights, shape[axis_at] // blocks).reshape([-1 if axis == axis_at else 1 for axis in range(len(shape))])
    return level


def profile(number_of, total, limit, slope):
    loads = [(1 << 20) // math.isqrt(grade ** slope) + 1 for grade in range(2, number_of + 1)]
    surplus, counts = total - limit - (number_of - 1), [1] * (number_of - 1)
    while surplus > 0:
        candidates = [i for i in range(number_of - 1) if counts[i] < limit]
        pool, budget = sum([loads[i] for i in candidates]), surplus
        for i in candidates:
            extra = min(limit - counts[i], max(1, budget * loads[i] // pool), surplus)
            counts[i] = counts[i] + extra
            surplus = surplus - extra
    return np.array([limit] + counts)


def ragged_sizes(rng, amount, total, most, lean):
    if amount == 2:
        one = jax.random.randint(rng, (), max(1, total - most), min(most, total - 1) + 1)
        return jnp.stack([one, total - one])
    lengths = jnp.asarray(profile(amount, total, most, lean), jnp.int32)
    couples = (amount - 1) // 2
    source_of, taker = lengths[1:1 + 2 * couples:2], lengths[2:2 + 2 * couples:2]
    margin = jnp.minimum(source_of - 1, most - taker)
    passed = jax.random.randint(jax.random.fold_in(rng, 1), (couples,), 0, 1 << 20) % (margin + 1)
    lengths = lengths.at[1:1 + 2 * couples:2].set(source_of - passed).at[2:2 + 2 * couples:2].set(taker + passed)
    return lengths[jax.random.permutation(jax.random.fold_in(rng, 2), amount)]


def normal_values(rng, shape, deviation, bound, shards=(), held_as=jnp.bfloat16):
    values = deviation * jax.random.normal(rng, shape, jnp.float32)
    if shards:
        values = values * steps_of(rng, shape, shards, -0.22, 0.18)
    return jnp.clip(values, -bound, bound).astype(held_as)


def setup_inputs(seed: int = 0) -> dict:
    key_list = jax.random.split(jax.random.key(seed), 6)
    return {
        "query": draw_query(jax.random.fold_in(key_list[5], 71), 0),
        "key": draw_key(jax.random.fold_in(key_list[5], 71), 0),
        "value": normal_values(key_list[2], (TOKENS, KV_HEADS * HEAD_DIM), 1.0, 6.0, ((0, 768),)),
        "grad_out": normal_values(key_list[3], (TOKENS, Q_HEADS * HEAD_DIM), 1.0, 6.0, ((0, 768),)),
        "segment_ids": jnp.searchsorted(jnp.cumsum(ragged_sizes(key_list[4], DOCS, TOKENS, DOC_MOST, 2)), jnp.arange(TOKENS), side="right").astype(jnp.int32),
    }


logit_scale = 168.0 ** -0.5


def reference(query, key, value, grad_out, segment_ids):
    span = WINDOW + TOK_DEV
    blocks = TOKENS // TOK_DEV
    group = Q_HEADS // KV_HEADS
    front = jnp.zeros((WINDOW, KV_HEADS * HEAD_DIM), key.dtype)
    key_pad = jnp.concatenate([front, key], axis=0)
    value_pad = jnp.concatenate([front, value], axis=0)
    seg_pad = jnp.concatenate([jnp.full((WINDOW,), -1, jnp.int32), segment_ids.astype(jnp.int32)])
    offsets_q = jnp.arange(TOK_DEV, dtype=jnp.int32)
    offsets_k = jnp.arange(span, dtype=jnp.int32)
    distance = WINDOW + offsets_q[:, None] - offsets_k[None, :]

    def step(carry, index):
        grad_k_pad, grad_v_pad = carry
        start = (index * TOK_DEV).astype(jnp.int32)
        query_block = lax.dynamic_slice_in_dim(query, start, TOK_DEV, 0).reshape(TOK_DEV, KV_HEADS, group, HEAD_DIM).astype(jnp.float32)
        g_blk = lax.dynamic_slice_in_dim(grad_out, start, TOK_DEV, 0).reshape(TOK_DEV, KV_HEADS, group, HEAD_DIM).astype(jnp.float32)
        key_block = lax.dynamic_slice_in_dim(key_pad, start, span, 0).reshape(span, KV_HEADS, HEAD_DIM).astype(jnp.float32)
        value_block = lax.dynamic_slice_in_dim(value_pad, start, span, 0).reshape(span, KV_HEADS, HEAD_DIM).astype(jnp.float32)
        seg_q = lax.dynamic_slice_in_dim(segment_ids.astype(jnp.int32), start, TOK_DEV, 0)
        seg_k = lax.dynamic_slice_in_dim(seg_pad, start, span, 0)
        allowed = (seg_q[:, None] == seg_k[None, :]) & (distance >= 0) & (distance < WINDOW)
        unscaled_scores = jnp.einsum("nobi,koi->obnk", query_block, key_block) * logit_scale
        masked = jnp.where(allowed, unscaled_scores, -jnp.inf)
        top = jnp.max(masked, axis=-1, keepdims=True)
        expo = jnp.where(allowed, jnp.exp(masked - top), 0.0)
        denominator_sum = jnp.sum(expo, axis=-1, keepdims=True)
        attention_weight = lax.optimization_barrier(expo.astype(jnp.bfloat16)).astype(jnp.float32)
        output_rows = jnp.einsum("xypq,qxa->xypa", attention_weight, value_block) / denominator_sum
        out_half = lax.optimization_barrier(output_rows.astype(jnp.bfloat16))
        grouped_output_gradient = jnp.transpose(g_blk, (1, 2, 0, 3))
        grouped_queries = jnp.transpose(query_block, (1, 2, 0, 3))
        delta = jnp.sum(grouped_output_gradient * out_half.astype(jnp.float32), axis=-1, keepdims=True)
        probabilities = expo / denominator_sum
        probability_gradient = jnp.einsum("pmcz,fpz->pmcf", grouped_output_gradient, value_block)
        score_gradient = lax.optimization_barrier((probabilities * (probability_gradient - delta)).astype(jnp.bfloat16)).astype(jnp.float32)
        query_gradient = jnp.einsum("xypq,qxa->xypa", score_gradient, key_block) * logit_scale
        key_gradient_partial = jnp.einsum("ihjm,ihjx->mix", score_gradient, grouped_queries) * logit_scale
        probabilities_bf16 = lax.optimization_barrier(probabilities.astype(jnp.bfloat16)).astype(jnp.float32)
        value_gradient_partial = jnp.einsum("ihjm,ihjx->mix", probabilities_bf16, grouped_output_gradient)
        old_k = lax.dynamic_slice_in_dim(grad_k_pad, start, span, 0)
        old_v = lax.dynamic_slice_in_dim(grad_v_pad, start, span, 0)
        grad_k_pad = lax.dynamic_update_slice_in_dim(grad_k_pad, old_k + key_gradient_partial.reshape(span, KV_HEADS * HEAD_DIM), start, 0)
        grad_v_pad = lax.dynamic_update_slice_in_dim(grad_v_pad, old_v + value_gradient_partial.reshape(span, KV_HEADS * HEAD_DIM), start, 0)
        out_rows = jnp.transpose(out_half, (2, 0, 1, 3)).reshape(TOK_DEV, Q_HEADS * HEAD_DIM)
        grad_q_rows = jnp.transpose(query_gradient, (2, 0, 1, 3)).reshape(TOK_DEV, Q_HEADS * HEAD_DIM).astype(jnp.bfloat16)
        return (grad_k_pad, grad_v_pad), (out_rows, grad_q_rows)

    zeros_pad = jnp.zeros((TOKENS + WINDOW, KV_HEADS * HEAD_DIM), jnp.float32)
    (grad_k_pad, grad_v_pad), (out_all, grad_q_all) = lax.scan(step, (zeros_pad, zeros_pad), jnp.arange(blocks, dtype=jnp.int32))
    attn_out = out_all.reshape(TOKENS, Q_HEADS * HEAD_DIM)
    grad_query = grad_q_all.reshape(TOKENS, Q_HEADS * HEAD_DIM)
    grad_key = grad_k_pad[WINDOW:].astype(jnp.bfloat16)
    grad_value = grad_v_pad[WINDOW:].astype(jnp.bfloat16)
    return (attn_out, grad_query, grad_key, grad_value)
```

```python
import functools
import math

import jax
import jax.numpy as jnp
from jax import lax
from jax.experimental import pallas as pl
from jax.experimental.pallas import tpu as pltpu
from jax.sharding import PartitionSpec as P

MESH = pl.DeviceIdType.MESH
D = 128
WINDOW = 1024
SCALE = 168.0 ** -0.5
C2 = SCALE * math.log2(math.e)
NEG = -1e30
F32 = jnp.float32
BF16 = jnp.bfloat16
B = 256
PIECE = 64
TILES = 5
ORDER = ((2, 0), (2, 1), (1, 0), (1, 1), (3, 0), (3, 1), (0, 1))
ARRIVE = ((0, 0), (0, 1), (1, 0), (3, 0), (1, 1), (3, 1), (2, 0), (2, 1))


def dot_nt(a, b):
    return lax.dot_general(a, b, (((1,), (1,)), ((), ())), preferred_element_type=F32)


def dot_nn(a, b):
    return jnp.dot(a, b, preferred_element_type=F32)


def wide(x):
    return jnp.concatenate([x, x], axis=1)


def kernel(pipe, q_ref, k_ref, v_ref, g_ref, seg_ref, o_out, dq_out, dk_out, dv_out,
           qst, gst, kbuf, vbuf, bias, pbuf, mtile, mrun, lrun, acc, delta,
           qT, gT, dkT, dvT, obuf, dqbuf, snd2, rcv2, snd1, rcv1, fin,
           in_send, in_recv, own_sem, halo_send, halo_recv, ret_send, ret_recv,
           out_send, out_recv, out_own):
    p = lax.axis_index("pipe")
    t = lax.axis_index("tensor")
    core = p % 2
    chip = p // 2
    nxt = ((p + 2) % pipe, t)
    prv = ((p + pipe - 2) % pipe, t)
    head = 2 * t + core

    def peer(dx, dc):
        c = (core + dc) % 2
        return c, (t + dx) % 4

    def source(dx, dc):
        c = (core + dc) % 2
        return c, (t + 4 - dx) % 4

    barrier = pltpu.get_barrier_semaphore()
    for dx, dc in ORDER:
        c, x = peer(dx, dc)
        pl.semaphore_signal(barrier, inc=1, device_id=(chip * 2 + c, x), device_id_type=MESH)
    pl.semaphore_signal(barrier, inc=1, device_id=nxt, device_id_type=MESH)
    pl.semaphore_signal(barrier, inc=1, device_id=prv, device_id_type=MESH)
    pl.semaphore_wait(barrier, 9)

    def src_of(a, head_of):
        if a == 0:
            return k_ref.at[:, pl.ds(pl.multiple_of(head_of * D, D), D)]
        if a == 1:
            return v_ref.at[:, pl.ds(pl.multiple_of(head_of * D, D), D)]
        h = a % 2
        ref = q_ref if a < 4 else g_ref
        return ref.at[:, pl.ds(pl.multiple_of((2 * head_of + h) * D, D), D)]

    def dst_of(a, c, x):
        if a < 2:
            ref = kbuf if a == 0 else vbuf
            return ref.at[pl.ds(pl.multiple_of(4 * B + c * B + x * PIECE, PIECE), PIECE), :]
        h = a % 2
        ref = qst if a < 4 else gst
        return ref.at[c, pl.ds(pl.multiple_of(h * B + x * PIECE, PIECE), PIECE), :]

    def exchange(a, dx, dc, landing):
        c, x = peer(dx, dc)
        sc, sx = source(dx, dc) if landing else (core, t)
        return pltpu.make_async_remote_copy(
            src_ref=src_of(a, 2 * x + c), dst_ref=dst_of(a, sc, sx),
            send_sem=in_send.at[a, dx, dc], recv_sem=in_recv.at[a, dx, dc],
            device_id=(chip * 2 + c, x), device_id_type=MESH)

    def own(a):
        return pltpu.make_async_copy(src_of(a, head), dst_of(a, core, t), own_sem.at[a])

    def rows_at(ref, block, c, x):
        return ref.at[pl.ds(pl.multiple_of(block * 2 * B + c * B + x * PIECE, PIECE), PIECE), :]

    def halo(hop, a, dx, dc):
        c, x = source(dx, dc)
        ref = kbuf if a == 0 else vbuf
        if hop == 0 and (dx, dc) == (0, 0):
            src = src_of(a, head)
        else:
            src = rows_at(ref, 2 - hop, c, x)
        return pltpu.make_async_remote_copy(
            src_ref=src, dst_ref=rows_at(ref, 1 - hop, c, x),
            send_sem=halo_send.at[hop, a, dx, dc], recv_sem=halo_recv.at[hop, a, dx, dc],
            device_id=nxt, device_id_type=MESH)

    for a in range(6):
        for dx, dc in ORDER:
            exchange(a, dx, dc, False).start()
        own(a).start()
        if a < 2:
            halo(0, a, 0, 0).start()

    row = lax.broadcasted_iota(jnp.int32, (B, D), 0)
    col = lax.broadcasted_iota(jnp.int32, (B, D), 1)

    def seg_row(r):
        at = chip * 4 - 8 + r
        s = seg_ref[pl.ds(jnp.maximum(at, 0), 1), :]
        return jnp.where(at >= 0, s, -1)

    for b in range(2):
        qcols = []
        for part in range(2):
            s = jnp.broadcast_to(seg_row(8 + 2 * b + part), (D, D))
            qcols.append(jnp.transpose(s))
        qseg = jnp.concatenate(qcols, axis=0)

        def mask_tile(l, carry):
            i = b + l
            for part in range(2):
                kseg = jnp.broadcast_to(seg_row(2 * i + part), (B, D))
                gap = row - col + (b * B + 4 * B - i * B - part * D)
                ok = (kseg == qseg) & (gap >= 0) & (gap < WINDOW)
                bias[b, l, :, part * D:(part + 1) * D] = jnp.where(ok, 0.0, NEG)
            return carry

        lax.fori_loop(0, TILES, mask_tile, 0)

    mrun[...] = jnp.full(mrun.shape, NEG, F32)
    lrun[...] = jnp.zeros(lrun.shape, F32)
    acc[...] = jnp.zeros(acc.shape, F32)

    for a in range(2):
        own(a).wait()
        for dx, dc in ARRIVE[1:]:
            exchange(a, dx, dc, True).wait_recv()
            halo(0, a, dx, dc).start()

    def pass_on(a):
        for dx, dc in ARRIVE:
            halo(0, a, dx, dc).wait_recv()
            halo(1, a, dx, dc).start()

    def arrived(a):
        own(a).wait()
        for dx, dc in ARRIVE[1:]:
            exchange(a, dx, dc, True).wait_recv()

    def k_tile(i):
        return kbuf[pl.ds(pl.multiple_of(i * B, B), B), :]

    def v_tile(i):
        return vbuf[pl.ds(pl.multiple_of(i * B, B), B), :]

    def forward(b, i):
        l = i - b
        n = b * TILES + l
        s = dot_nt(qst[b], k_tile(i)) * C2
        bias_t = bias[b, l]
        s = s + jnp.concatenate([bias_t, bias_t], axis=0)
        m_old = mrun[b]
        m_new = jnp.maximum(m_old, jnp.max(s, axis=1, keepdims=True))
        e = jnp.exp2(s - wide(m_new))
        alpha = jnp.exp2(m_old - m_new)
        mrun[b] = m_new
        mtile[n] = m_new
        lrun[b] = lrun[b] * alpha + jnp.sum(e, axis=1, keepdims=True)
        e16 = e.astype(BF16)
        pbuf[n] = e16
        acc[b] = acc[b] * alpha + dot_nn(e16, v_tile(i))

    pass_on(0)
    for a in (2, 3):
        arrived(a)

    def phase1(n, carry):
        forward(jnp.minimum(n, 1), 4 + n % 2)
        return carry

    lax.fori_loop(0, 3, phase1, 0)
    pass_on(1)

    def phase2(n, carry):
        forward(n // 2, 3 - n % 2)
        return carry

    lax.fori_loop(0, 4, phase2, 0)
    for a in (4, 5):
        arrived(a)
    for b in range(2):
        qT[b] = jnp.transpose(qst[b].astype(F32)).astype(BF16)
        gT[b] = jnp.transpose(gst[b].astype(F32)).astype(BF16)
    dkT[...] = jnp.zeros(dkT.shape, F32)
    dvT[...] = jnp.zeros(dvT.shape, F32)
    for a in range(2):
        for dx, dc in ARRIVE:
            halo(1, a, dx, dc).wait_recv()

    def phase3(n, carry):
        forward(n // 2, 1 - n % 2)
        return carry

    lax.fori_loop(0, 3, phase3, 0)

    def out_src(a, c, x):
        if a < 4:
            ref = obuf if a < 2 else dqbuf
            return ref.at[c, pl.ds(pl.multiple_of((a % 2) * B + x * PIECE, PIECE), PIECE), :]
        return fin.at[a - 4, c, pl.ds(pl.multiple_of(x * PIECE, PIECE), PIECE), :]

    def out_dst(a, head_of):
        if a < 4:
            ref = o_out if a < 2 else dq_out
            return ref.at[:, pl.ds(pl.multiple_of((2 * head_of + a % 2) * D, D), D)]
        ref = dk_out if a == 4 else dv_out
        return ref.at[:, pl.ds(pl.multiple_of(head_of * D, D), D)]

    def give(a, dx, dc, landing):
        c, x = peer(dx, dc)
        if landing:
            sc, sx = source(dx, dc)
            from_head = 2 * sx + sc
        else:
            from_head = head
        return pltpu.make_async_remote_copy(
            src_ref=out_src(a, c, x), dst_ref=out_dst(a, from_head),
            send_sem=out_send.at[a, dx, dc], recv_sem=out_recv.at[a, dx, dc],
            device_id=(chip * 2 + c, x), device_id_type=MESH)

    def keep(a):
        return pltpu.make_async_copy(out_src(a, core, t), out_dst(a, head), out_own.at[a])

    def give_all(a):
        for dx, dc in ORDER:
            give(a, dx, dc, False).start()
        keep(a).start()

    for b in range(2):
        linv = 1.0 / lrun[b]
        lrun[b] = linv
        o16 = (acc[b] * linv).astype(BF16)
        obuf[b] = o16
        d = jnp.sum(gst[b].astype(F32) * o16.astype(F32), axis=1, keepdims=True)
        delta[b] = jnp.broadcast_to(d, (2 * B, D))
    acc[...] = jnp.zeros(acc.shape, F32)

    def backward(b, i):
        n = b * TILES + i - b
        r = jnp.exp2(mtile[n] - mrun[b]) * lrun[b]
        prob = pbuf[n].astype(F32) * wide(r)
        dp = dot_nt(gst[b], v_tile(i))
        ds = (prob * (dp - wide(delta[b]))).astype(BF16)
        dvT[i] += dot_nn(gT[b], prob.astype(BF16))
        dkT[i] += dot_nn(qT[b], ds)
        acc[b] += dot_nn(ds, k_tile(i))

    def back(hop, i, a):
        s, r = (snd2, rcv2) if hop == 0 else (snd1, rcv1)
        return pltpu.make_async_remote_copy(
            src_ref=s.at[i, a], dst_ref=r.at[i, a],
            send_sem=ret_send.at[hop, i, a], recv_sem=ret_recv.at[hop, i, a],
            device_id=prv, device_id_type=MESH)

    def phase4(n, carry):
        backward(n // 2, (n + 1) // 2)
        return carry

    backward(0, 0)
    for a, ref in ((0, dkT), (1, dvT)):
        snd2[0, a] = ref[0].astype(BF16)
        back(0, 0, a).start()
    for a in range(2):
        give_all(a)

    def pair(n, carry):
        backward(n % 2, 1 + n // 2)
        return carry

    lax.fori_loop(0, 2, pair, 0)
    for a, ref in ((0, dkT), (1, dvT)):
        snd2[1, a] = ref[1].astype(BF16)
        back(0, 1, a).start()
    lax.fori_loop(2, 6, pair, 0)
    for i in range(2):
        for a, ref in ((0, dkT), (1, dvT)):
            back(0, i, a).wait_recv()
            snd1[i, a] = (ref[2 + i] + rcv2[i, a].astype(F32)).astype(BF16)
            back(1, i, a).start()
    lax.fori_loop(6, 8, pair, 0)
    backward(1, 5)
    for b in range(2):
        dqbuf[b] = (acc[b] * SCALE).astype(BF16)
    for a in (2, 3):
        give_all(a)
    for i in range(2):
        for a, ref in ((0, dkT), (1, dvT)):
            back(1, i, a).wait_recv()
            total = ref[4 + i] + rcv1[i, a].astype(F32)
            if a == 0:
                total = total * SCALE
            fin[a, i] = jnp.transpose(total).astype(BF16)
    for a in (4, 5):
        give_all(a)

    for a in range(6):
        for dx, dc in ORDER:
            exchange(a, dx, dc, False).wait_send()
            give(a, dx, dc, False).wait_send()
            give(a, dx, dc, True).wait_recv()
        keep(a).wait()
    for hop in range(2):
        for a in range(2):
            for dx, dc in ARRIVE:
                halo(hop, a, dx, dc).wait_send()
            for i in range(2):
                back(hop, i, a).wait_send()


def body(pipe, query, key, value, grad_out, segment_ids):
    seg = segment_ids.reshape(-1, D)
    anyspace = pl.BlockSpec(memory_space=pl.ANY)
    dma = pltpu.SemaphoreType.DMA
    return pl.pallas_call(
        functools.partial(kernel, pipe),
        out_shape=tuple(jax.ShapeDtypeStruct(x.shape, BF16) for x in (query, query, key, value)),
        in_specs=[anyspace] * 4 + [pl.BlockSpec(memory_space=pltpu.VMEM)],
        out_specs=(anyspace,) * 4,
        scratch_shapes=[
            pltpu.VMEM((2, 2 * B, D), BF16),
            pltpu.VMEM((2, 2 * B, D), BF16),
            pltpu.VMEM((6 * B, D), BF16),
            pltpu.VMEM((6 * B, D), BF16),
            pltpu.VMEM((2, TILES, B, B), F32),
            pltpu.VMEM((2 * TILES, 2 * B, B), BF16),
            pltpu.VMEM((2 * TILES, 2 * B, D), F32),
            pltpu.VMEM((2, 2 * B, D), F32),
            pltpu.VMEM((2, 2 * B, D), F32),
            pltpu.VMEM((2, 2 * B, D), F32),
            pltpu.VMEM((2, 2 * B, D), F32),
            pltpu.VMEM((2, D, 2 * B), BF16),
            pltpu.VMEM((2, D, 2 * B), BF16),
            pltpu.VMEM((6, D, B), F32),
            pltpu.VMEM((6, D, B), F32),
            pltpu.VMEM((2, 2 * B, D), BF16),
            pltpu.VMEM((2, 2 * B, D), BF16),
            pltpu.VMEM((2, 2, D, B), BF16),
            pltpu.VMEM((2, 2, D, B), BF16),
            pltpu.VMEM((2, 2, D, B), BF16),
            pltpu.VMEM((2, 2, D, B), BF16),
            pltpu.VMEM((2, 2, B, D), BF16),
            dma((6, 4, 2)), dma((6, 4, 2)), dma((6,)),
            dma((2, 2, 4, 2)), dma((2, 2, 4, 2)),
            dma((2, 2, 2)), dma((2, 2, 2)),
            dma((6, 4, 2)), dma((6, 4, 2)), dma((6,)),
        ],
        compiler_params=pltpu.CompilerParams(
            collective_id=0, has_side_effects=True, vmem_limit_bytes=40 * 1024 * 1024),
    )(query, key, value, grad_out, seg)


def solution(mesh):
    spec = P(("pipe", "tensor"), None)
    return jax.shard_map(
        functools.partial(body, mesh.shape["pipe"]),
        mesh=mesh,
        in_specs=(spec,) * 4 + (P(),),
        out_specs=(spec,) * 4,
        check_vma=False,
    )
```

```python
import functools
import math

import jax
import jax.numpy as jnp
from jax import lax
from jax.experimental import pallas as pl
from jax.experimental.pallas import tpu as pltpu
from jax.sharding import PartitionSpec as P

MESH = pl.DeviceIdType.MESH
D = 128
WINDOW = 1024
SCALE = 168.0 ** -0.5
C2 = SCALE * math.log2(math.e)
NEG = -1e30
F32 = jnp.float32
BF16 = jnp.bfloat16
B = 256
PIECE = 64
TILES = 5


def dot_nt(a, b):
    return lax.dot_general(a, b, (((1,), (1,)), ((), ())), preferred_element_type=F32)


def dot_nn(a, b):
    return jnp.dot(a, b, preferred_element_type=F32)


def wide(x):
    return jnp.concatenate([x, x], axis=1)


def kernel(pipe, q_ref, k_ref, v_ref, g_ref, seg_hbm, o_out, dq_out, dk_out, dv_out,
           seg_ref, qst, gst, kbuf, vbuf, bias, pbuf, mtile, mrun, lrun, acc, delta,
           qT, gT, dkT, dvT, obuf, dqbuf, snd2, rcv2, snd1, rcv1, fin,
           seg_sem, in_send, in_recv, own_sem, halo_send, halo_recv, ret_send, ret_recv,
           out_send, out_recv, out_own):
    p = lax.axis_index("pipe")
    t = lax.axis_index("tensor")
    core = p % 2
    other = 1 - core
    chip = p // 2
    chips = pipe // 2
    nxt = ((p + 2) % pipe, t)
    prv = ((p + pipe - 2) % pipe, t)
    head = 2 * t + core
    has_prev, has_prev2, has_next = chip >= 1, chip >= 2, chip < chips - 1
    has_both = has_prev & has_next
    FAR = [(dx, c) for dx in (2, 1, 3) for c in range(2)]
    ALL = [(0, other)] + FAR

    seg_copy = pltpu.make_async_copy(seg_hbm, seg_ref, seg_sem)
    seg_copy.start()
    barrier = pltpu.get_barrier_semaphore()
    for dx, c in ALL:
        pl.semaphore_signal(barrier, inc=1, device_id=(chip * 2 + c, (t + dx) % 4), device_id_type=MESH)

    @pl.when(has_next)
    def _():
        pl.semaphore_signal(barrier, inc=1, device_id=nxt, device_id_type=MESH)

    @pl.when(has_prev)
    def _():
        pl.semaphore_signal(barrier, inc=1, device_id=prv, device_id_type=MESH)

    pl.semaphore_wait(barrier, 9 - (chip == 0).astype(jnp.int32) - (chip == chips - 1).astype(jnp.int32))

    def src_of(a, head_of):
        if a == 0:
            return k_ref.at[:, pl.ds(pl.multiple_of(head_of * D, D), D)]
        if a == 1:
            return v_ref.at[:, pl.ds(pl.multiple_of(head_of * D, D), D)]
        h = a % 2
        ref = q_ref if a < 4 else g_ref
        return ref.at[:, pl.ds(pl.multiple_of((2 * head_of + h) * D, D), D)]

    def dst_of(a, c, x):
        if a < 2:
            ref = kbuf if a == 0 else vbuf
            return ref.at[pl.ds(pl.multiple_of(4 * B + c * B + x * PIECE, PIECE), PIECE), :]
        h = a % 2
        ref = qst if a < 4 else gst
        return ref.at[c, pl.ds(pl.multiple_of(h * B + x * PIECE, PIECE), PIECE), :]

    def exchange(a, dx, c):
        x = (t + dx) % 4
        return pltpu.make_async_remote_copy(
            src_ref=src_of(a, 2 * x + c), dst_ref=dst_of(a, core, t),
            send_sem=in_send.at[a, dx, c], recv_sem=in_recv.at[a, dx, core],
            device_id=(chip * 2 + c, x), device_id_type=MESH)

    def exchanged(a, dx, c):
        x = (t + 4 - dx) % 4
        return pltpu.make_async_remote_copy(
            src_ref=src_of(a, head), dst_ref=dst_of(a, c, x),
            send_sem=in_send.at[a, dx, c], recv_sem=in_recv.at[a, dx, c],
            device_id=(chip * 2 + c, x), device_id_type=MESH)

    def own(a):
        return pltpu.make_async_copy(src_of(a, head), dst_of(a, core, t), own_sem.at[a])

    def rows_at(ref, block, c, x):
        return ref.at[pl.ds(pl.multiple_of(block * 2 * B + c * B + x * PIECE, PIECE), PIECE), :]

    def halo(hop, a, dx, c):
        x = (t + 4 - dx) % 4
        ref = kbuf if a == 0 else vbuf
        return pltpu.make_async_remote_copy(
            src_ref=rows_at(ref, 2 - hop, c, x), dst_ref=rows_at(ref, 1 - hop, c, x),
            send_sem=halo_send.at[hop, a, dx, c], recv_sem=halo_recv.at[hop, a, dx, c],
            device_id=nxt, device_id_type=MESH)

    for a in range(6):
        exchange(a, 0, other).start()
        own(a).start()
    for a in range(6):
        for dx, c in FAR:
            exchange(a, dx, c).start()

    def zero_block(block):
        kbuf[block * 2 * B:(block + 1) * 2 * B, :] = jnp.zeros((2 * B, D), BF16)
        vbuf[block * 2 * B:(block + 1) * 2 * B, :] = jnp.zeros((2 * B, D), BF16)

    @pl.when(chip == 0)
    def _():
        zero_block(1)

    @pl.when(chip <= 1)
    def _():
        zero_block(0)

    seg_copy.wait()

    row = lax.broadcasted_iota(jnp.int32, (B, D), 0)
    col = lax.broadcasted_iota(jnp.int32, (B, D), 1)

    def seg_row(r):
        at = chip * 4 - 8 + r
        s = seg_ref[pl.ds(jnp.maximum(at, 0), 1), :]
        return jnp.where(at >= 0, s, -1)

    for b in range(2):
        qcols = []
        for part in range(2):
            s = jnp.broadcast_to(seg_row(8 + 2 * b + part), (D, D))
            qcols.append(jnp.transpose(s))
        qseg = jnp.concatenate(qcols, axis=0)

        def mask_tile(l, carry):
            i = b + l
            for part in range(2):
                kseg = jnp.broadcast_to(seg_row(2 * i + part), (B, D))
                gap = row - col + (b * B + 4 * B - i * B - part * D)
                ok = (kseg == qseg) & (gap >= 0) & (gap < WINDOW)
                bias[b, l, :, part * D:(part + 1) * D] = jnp.where(ok, 0.0, NEG)
            return carry

        lax.fori_loop(0, TILES, mask_tile, 0)

    mrun[...] = jnp.full(mrun.shape, NEG, F32)
    lrun[...] = jnp.zeros(lrun.shape, F32)
    acc[...] = jnp.zeros(acc.shape, F32)

    NEAR = [(0, 0), (0, 1), (1, 0), (3, 0), (1, 1), (3, 1), (2, 0), (2, 1)]

    def arrived(a, dx, c):
        if dx == 0:
            @pl.when(core == c)
            def _():
                own(a).wait()

            @pl.when(core != c)
            def _():
                exchanged(a, 0, c).wait_recv()
        else:
            exchanged(a, dx, c).wait_recv()

    for a in range(2):
        for dx, c in NEAR:
            arrived(a, dx, c)

            @pl.when(has_next)
            def _():
                halo(0, a, dx, c).start()

    for c in (1, 0):
        for a in range(2):
            for dx in (0, 1, 3, 2):
                @pl.when(has_prev)
                def _():
                    halo(0, a, dx, c).wait_recv()

                @pl.when(has_both)
                def _():
                    halo(1, a, dx, c).start()

    def k_tile(i):
        return kbuf[pl.ds(pl.multiple_of(i * B, B), B), :]

    def v_tile(i):
        return vbuf[pl.ds(pl.multiple_of(i * B, B), B), :]

    def forward(b, i):
        l = i - b
        n = b * TILES + l
        s = dot_nt(qst[b], k_tile(i)) * C2
        bias_t = bias[b, l]
        s = s + jnp.concatenate([bias_t, bias_t], axis=0)
        m_old = mrun[b]
        m_new = jnp.maximum(m_old, jnp.max(s, axis=1, keepdims=True))
        e = jnp.exp2(s - wide(m_new))
        alpha = jnp.exp2(m_old - m_new)
        mrun[b] = m_new
        mtile[n] = m_new
        lrun[b] = lrun[b] * alpha + jnp.sum(e, axis=1, keepdims=True)
        e16 = e.astype(BF16)
        pbuf[n] = e16
        acc[b] = acc[b] * alpha + dot_nn(e16, v_tile(i))

    for a in (2, 3):
        for dx, c in NEAR:
            arrived(a, dx, c)

    def phase1(n, carry):
        forward(jnp.minimum(n, 1), 4 + n % 2)
        return carry

    lax.fori_loop(0, 3, phase1, 0)

    def phase2(n, carry):
        forward(n // 2, 3 - n % 2)
        return carry

    lax.fori_loop(0, 4, phase2, 0)
    for a in (4, 5):
        for dx, c in NEAR:
            arrived(a, dx, c)
    for b in range(2):
        qT[b] = jnp.transpose(qst[b].astype(F32)).astype(BF16)
        gT[b] = jnp.transpose(gst[b].astype(F32)).astype(BF16)
    dkT[...] = jnp.zeros(dkT.shape, F32)
    dvT[...] = jnp.zeros(dvT.shape, F32)

    def finish(b):
        linv = 1.0 / lrun[b]
        lrun[b] = linv
        o16 = (acc[b] * linv).astype(BF16)
        obuf[b] = o16
        d = jnp.sum(gst[b].astype(F32) * o16.astype(F32), axis=1, keepdims=True)
        delta[b] = jnp.broadcast_to(d, (2 * B, D))
        acc[b] = jnp.zeros((2 * B, D), F32)

    for c in (1, 0):
        @pl.when(has_prev2)
        def _():
            for a in range(2):
                for dx in range(4):
                    halo(1, a, dx, c).wait_recv()

        if c == 1:
            def phase3(n, carry):
                forward(n, 1)
                return carry

            lax.fori_loop(0, 2, phase3, 0)
            finish(1)
        else:
            forward(0, 0)
            finish(0)

    def out_src(a, c, x):
        if a < 4:
            ref = obuf if a < 2 else dqbuf
            return ref.at[c, pl.ds(pl.multiple_of((a % 2) * B + x * PIECE, PIECE), PIECE), :]
        return fin.at[a - 4, c, pl.ds(pl.multiple_of(x * PIECE, PIECE), PIECE), :]

    def out_dst(a, head_of):
        if a < 4:
            ref = o_out if a < 2 else dq_out
            return ref.at[:, pl.ds(pl.multiple_of((2 * head_of + a % 2) * D, D), D)]
        ref = dk_out if a == 4 else dv_out
        return ref.at[:, pl.ds(pl.multiple_of(head_of * D, D), D)]

    def give(a, dx, c):
        x = (t + dx) % 4
        return pltpu.make_async_remote_copy(
            src_ref=out_src(a, c, x), dst_ref=out_dst(a, head),
            send_sem=out_send.at[a, dx, c], recv_sem=out_recv.at[a, dx, core],
            device_id=(chip * 2 + c, x), device_id_type=MESH)

    def given(a, dx, c):
        x = (t + 4 - dx) % 4
        return pltpu.make_async_remote_copy(
            src_ref=out_src(a, core, t), dst_ref=out_dst(a, 2 * x + c),
            send_sem=out_send.at[a, dx, c], recv_sem=out_recv.at[a, dx, c],
            device_id=(chip * 2 + c, x), device_id_type=MESH)

    def keep(a):
        return pltpu.make_async_copy(out_src(a, core, t), out_dst(a, head), out_own.at[a])

    def give_all(arrays):
        for a in arrays:
            for dx, c in FAR:
                give(a, dx, c).start()
            give(a, 0, other).start()
            keep(a).start()

    def backward(b, i):
        n = b * TILES + i - b
        r = jnp.exp2(mtile[n] - mrun[b]) * lrun[b]
        prob = pbuf[n].astype(F32) * wide(r)
        dp = dot_nt(gst[b], v_tile(i))
        ds = (prob * (dp - wide(delta[b]))).astype(BF16)
        dvT[i] += dot_nn(gT[b], prob.astype(BF16))
        dkT[i] += dot_nn(qT[b], ds)
        acc[b] += dot_nn(ds, k_tile(i))

    def back(hop, i, a):
        s, r = (snd2, rcv2) if hop == 0 else (snd1, rcv1)
        return pltpu.make_async_remote_copy(
            src_ref=s.at[i, a], dst_ref=r.at[i, a],
            send_sem=ret_send.at[hop, i, a], recv_sem=ret_recv.at[hop, i, a],
            device_id=prv, device_id_type=MESH)

    def send_back(hop, i):
        for a, ref in ((0, dkT), (1, dvT)):
            if hop == 0:
                snd2[i, a] = ref[i].astype(BF16)

                @pl.when(has_prev2)
                def _():
                    back(0, i, a).start()
            else:
                @pl.when(has_both)
                def _():
                    back(0, i, a).wait_recv()
                    snd1[i, a] = (ref[2 + i] + rcv2[i, a].astype(F32)).astype(BF16)

                @pl.when(chip == chips - 1)
                def _():
                    snd1[i, a] = ref[2 + i].astype(BF16)

                @pl.when(has_prev)
                def _():
                    back(1, i, a).start()

    def pair(n, carry):
        backward(n % 2, 1 + n // 2)
        return carry

    backward(0, 0)
    send_back(0, 0)
    lax.fori_loop(0, 2, pair, 0)
    send_back(0, 1)
    give_all((0, 1))
    lax.fori_loop(2, 4, pair, 0)
    send_back(1, 0)
    lax.fori_loop(4, 6, pair, 0)
    send_back(1, 1)
    lax.fori_loop(6, 8, pair, 0)
    backward(1, 5)
    for b in range(2):
        dqbuf[b] = (acc[b] * SCALE).astype(BF16)
    give_all((2, 3))

    for i in range(2):
        for a, ref in ((0, dkT), (1, dvT)):
            factor = SCALE if a == 0 else 1.0

            @pl.when(has_next)
            def _():
                back(1, i, a).wait_recv()
                fin[a, i] = jnp.transpose((ref[4 + i] + rcv1[i, a].astype(F32)) * factor).astype(BF16)

            @pl.when(chip == chips - 1)
            def _():
                fin[a, i] = jnp.transpose(ref[4 + i] * factor).astype(BF16)

            for dx in (2, 1, 3):
                give(4 + a, dx, i).start()
    for a in (4, 5):
        give(a, 0, other).start()
        keep(a).start()

    for a in range(6):
        for dx, c in ALL:
            exchange(a, dx, c).wait_send()
            give(a, dx, c).wait_send()
            given(a, dx, c).wait_recv()
        keep(a).wait()

    @pl.when(has_next)
    def _():
        for a in range(2):
            for dx, c in NEAR:
                halo(0, a, dx, c).wait_send()

    @pl.when(has_both)
    def _():
        for a in range(2):
            for dx, c in NEAR:
                halo(1, a, dx, c).wait_send()

    for hop, cond in ((0, has_prev2), (1, has_prev)):
        @pl.when(cond)
        def _():
            for a in range(2):
                for i in range(2):
                    back(hop, i, a).wait_send()


def write_kernel(*refs):
    sems = refs[-1]
    copies = [pltpu.make_async_copy(refs[i], refs[4 + i], sems.at[i]) for i in range(4)]
    for copy in copies:
        copy.start()
    for copy in copies:
        copy.wait()


def body(pipe, query, key, value, grad_out, segment_ids):
    seg = segment_ids.reshape(-1, D)
    anyspace = pl.BlockSpec(memory_space=pl.ANY)
    dma = pltpu.SemaphoreType.DMA
    hbm = pl.BlockSpec(memory_space=pltpu.HBM)
    shapes = tuple(jax.ShapeDtypeStruct(x.shape, BF16) for x in (query, query, key, value))
    results = pl.pallas_call(
        functools.partial(kernel, pipe),
        out_shape=shapes,
        in_specs=[hbm] * 5,
        out_specs=(anyspace,) * 4,
        scratch_shapes=[
            pltpu.VMEM(seg.shape, jnp.int32),
            pltpu.VMEM((2, 2 * B, D), BF16),
            pltpu.VMEM((2, 2 * B, D), BF16),
            pltpu.VMEM((6 * B, D), BF16),
            pltpu.VMEM((6 * B, D), BF16),
            pltpu.VMEM((2, TILES, B, B), F32),
            pltpu.VMEM((2 * TILES, 2 * B, B), BF16),
            pltpu.VMEM((2 * TILES, 2 * B, D), F32),
            pltpu.VMEM((2, 2 * B, D), F32),
            pltpu.VMEM((2, 2 * B, D), F32),
            pltpu.VMEM((2, 2 * B, D), F32),
            pltpu.VMEM((2, 2 * B, D), F32),
            pltpu.VMEM((2, D, 2 * B), BF16),
            pltpu.VMEM((2, D, 2 * B), BF16),
            pltpu.VMEM((6, D, B), F32),
            pltpu.VMEM((6, D, B), F32),
            pltpu.VMEM((2, 2 * B, D), BF16),
            pltpu.VMEM((2, 2 * B, D), BF16),
            pltpu.VMEM((2, 2, D, B), BF16),
            pltpu.VMEM((2, 2, D, B), BF16),
            pltpu.VMEM((2, 2, D, B), BF16),
            pltpu.VMEM((2, 2, D, B), BF16),
            pltpu.VMEM((2, 2, B, D), BF16),
            dma(()), dma((6, 4, 2)), dma((6, 4, 2)), dma((6,)),
            dma((2, 2, 4, 2)), dma((2, 2, 4, 2)),
            dma((2, 2, 2)), dma((2, 2, 2)),
            dma((6, 4, 2)), dma((6, 4, 2)), dma((6,)),
        ],
        compiler_params=pltpu.CompilerParams(
            collective_id=0, has_side_effects=True, vmem_limit_bytes=40 * 1024 * 1024),
    )(*[pltpu.with_memory_space_constraint(x, pltpu.HBM) for x in (query, key, value, grad_out, seg)])
    return pl.pallas_call(
        write_kernel,
        out_shape=shapes,
        in_specs=[pl.BlockSpec(memory_space=pltpu.VMEM)] * 4,
        out_specs=(hbm,) * 4,
        scratch_shapes=[dma((4,))],
    )(*[pltpu.with_memory_space_constraint(x, pltpu.VMEM) for x in results])


def solution(mesh):
    spec = P(("pipe", "tensor"), None)
    return jax.shard_map(
        functools.partial(body, mesh.shape["pipe"]),
        mesh=mesh,
        in_specs=(spec,) * 4 + (P(),),
        out_specs=(spec,) * 4,
        check_vma=False,
    )
```

```python
import functools
import math

import jax
import jax.numpy as jnp
from jax import lax
from jax.experimental import pallas as pl
from jax.experimental.pallas import tpu as pltpu
from jax.sharding import PartitionSpec as P

MESH = pl.DeviceIdType.MESH
D = 128
WINDOW = 1024
SCALE = 168.0 ** -0.5
C2 = SCALE * math.log2(math.e)
NEG = -1e30
F32 = jnp.float32
BF16 = jnp.bfloat16
B = 256
PIECE = 64
TILES = 5


def dot_nt(a, b):
    return lax.dot_general(a, b, (((1,), (1,)), ((), ())), preferred_element_type=F32)


def dot_nn(a, b):
    return jnp.dot(a, b, preferred_element_type=F32)


def wide(x):
    return jnp.concatenate([x, x], axis=1)


def kernel(pipe, q_ref, k_ref, v_ref, g_ref, seg_hbm, o_out, dq_out, dk_out, dv_out,
           seg_ref, qst, gst, kbuf, vbuf, bias, pbuf, mtile, mrun, lrun, acc, delta,
           qT, gT, dkT, dvT, obuf, dqbuf, snd, rcv, fin,
           seg_sem, in_send, in_recv, own_sem, hop_send, hop_recv,
           out_send, out_recv, out_own):
    p = lax.axis_index("pipe")
    t = lax.axis_index("tensor")
    core = p % 2
    other = 1 - core
    chip = p // 2
    chips = pipe // 2
    nxt = ((p + 2) % pipe, t)
    prv = ((p + pipe - 2) % pipe, t)
    head = 2 * t + core
    has_prev, has_prev2, has_next = chip >= 1, chip >= 2, chip < chips - 1
    has_both = has_prev & has_next
    first, last = chip == 0, chip == chips - 1
    FAR = [(dx, c) for dx in (2, 1, 3) for c in range(2)]
    ALL = [(0, other)] + FAR

    seg_copy = pltpu.make_async_copy(seg_hbm, seg_ref, seg_sem)
    seg_copy.start()
    barrier = pltpu.get_barrier_semaphore()
    for dx, c in ALL:
        pl.semaphore_signal(barrier, inc=1, device_id=(chip * 2 + c, (t + dx) % 4), device_id_type=MESH)

    @pl.when(has_next)
    def _():
        pl.semaphore_signal(barrier, inc=1, device_id=nxt, device_id_type=MESH)

    @pl.when(has_prev)
    def _():
        pl.semaphore_signal(barrier, inc=1, device_id=prv, device_id_type=MESH)

    pl.semaphore_wait(barrier, 9 - (chip == 0).astype(jnp.int32) - (chip == chips - 1).astype(jnp.int32))

    def src_of(a, head_of):
        if a == 0:
            return k_ref.at[:, pl.ds(pl.multiple_of(head_of * D, D), D)]
        if a == 1:
            return v_ref.at[:, pl.ds(pl.multiple_of(head_of * D, D), D)]
        h = a % 2
        ref = q_ref if a < 4 else g_ref
        return ref.at[:, pl.ds(pl.multiple_of((2 * head_of + h) * D, D), D)]

    def rows_at(ref, tile, x):
        return ref.at[pl.ds(pl.multiple_of(tile * B + x * PIECE, PIECE), PIECE), :]

    def heads_at(a, tile, x):
        ref = qst if a < 4 else gst
        return ref.at[tile, pl.ds(pl.multiple_of((a % 2) * B + x * PIECE, PIECE), PIECE), :]

    def dst_of(a, c, x):
        if a < 2:
            return rows_at(kbuf if a == 0 else vbuf, 3 + c, x)
        return heads_at(a, 2 - 2 * c, x)

    def exchange(a, dx, c):
        x = (t + dx) % 4
        return pltpu.make_async_remote_copy(
            src_ref=src_of(a, 2 * x + c), dst_ref=dst_of(a, core, t),
            send_sem=in_send.at[a, dx, c], recv_sem=in_recv.at[a, dx, core],
            device_id=(chip * 2 + c, x), device_id_type=MESH)

    def exchanged(a, dx, c):
        x = (t + 4 - dx) % 4
        return pltpu.make_async_remote_copy(
            src_ref=src_of(a, head), dst_ref=dst_of(a, c, x),
            send_sem=in_send.at[a, dx, c], recv_sem=in_recv.at[a, dx, c],
            device_id=(chip * 2 + c, x), device_id_type=MESH)

    def own(a):
        return pltpu.make_async_copy(src_of(a, head), dst_of(a, core, t), own_sem.at[a])

    def hop(at, src, dst, dev):
        return pltpu.make_async_remote_copy(
            src_ref=src, dst_ref=dst, send_sem=hop_send.at[at], recv_sem=hop_recv.at[at],
            device_id=dev, device_id_type=MESH)

    def up(a, dx, c):
        ref, x = kbuf if a == 0 else vbuf, (t + 4 - dx) % 4
        return hop(a * 8 + dx * 2 + c, rows_at(ref, 3 + c, x), rows_at(ref, 1 + c, x), nxt)

    def up2(a, dx):
        ref, x = kbuf if a == 0 else vbuf, (t + 4 - dx) % 4
        return hop(16 + a * 4 + dx, rows_at(ref, 2, x), rows_at(ref, 0, x), nxt)

    def down(a, dx):
        x = (t + 4 - dx) % 4
        if a < 2:
            ref = kbuf if a == 0 else vbuf
            return hop(24 + a * 4 + dx, rows_at(ref, 3, x), rows_at(ref, 5, x), prv)
        return hop(24 + a * 4 + dx, heads_at(a, 2, x), heads_at(a, 1, x), prv)

    for a in range(6):
        exchange(a, 0, other).start()
        own(a).start()
    for a in range(6):
        for dx, c in FAR:
            exchange(a, dx, c).start()

    def zero_tile(i):
        kbuf[i * B:(i + 1) * B, :] = jnp.zeros((B, D), BF16)
        vbuf[i * B:(i + 1) * B, :] = jnp.zeros((B, D), BF16)

    @pl.when(first)
    def _():
        zero_tile(1)
        zero_tile(2)

    @pl.when(chip <= 1)
    def _():
        zero_tile(0)

    @pl.when(last)
    def _():
        zero_tile(5)
        qst[1] = jnp.zeros((2 * B, D), BF16)
        gst[1] = jnp.zeros((2 * B, D), BF16)

    def arrived(a, dx, c):
        if dx == 0:
            @pl.when(core == c)
            def _():
                own(a).wait()

            @pl.when(core != c)
            def _():
                exchanged(a, 0, c).wait_recv()
        else:
            exchanged(a, dx, c).wait_recv()

    STEPS = (0, 1, 3, 2)

    def masks():
        row = lax.broadcasted_iota(jnp.int32, (B, D), 0)
        col = lax.broadcasted_iota(jnp.int32, (B, D), 1)

        def seg_row(at):
            inside = (at >= 0) & (at < 4 * chips)
            r = seg_ref[pl.ds(jnp.minimum(jnp.maximum(at, 0), 4 * chips - 1), 1), :]
            return jnp.where(inside, r, -1)

        def seg_col(at):
            parts = [jnp.transpose(jnp.broadcast_to(seg_row(at + k), (D, D))) for k in range(2)]
            return jnp.concatenate(parts, axis=0)

        def mask(b, l, at, offset, qseg):
            for part in range(2):
                kseg = jnp.broadcast_to(seg_row(at + part), (B, D))
                gap = row - col + (offset - part * D)
                ok = (kseg == qseg) & (gap >= 0) & (gap < WINDOW)
                bias[b, l, :, part * D:(part + 1) * D] = jnp.where(ok, 0.0, NEG)

        for b in range(2):
            qseg = seg_col(4 * chip + 2 + 2 * b)

            def mask_tile(l, carry):
                mask(b, l, 4 * chip - 6 + 2 * (b + l), 4 * B - l * B, qseg)
                return carry

            lax.fori_loop(0, TILES, mask_tile, 0)

        @pl.when(first)
        def _():
            mask(2, 1, 4 * chip, 0, seg_col(4 * chip))

    for c in (1, 0):
        for a in range(2):
            for dx in STEPS:
                arrived(a, dx, c)

                @pl.when(has_next)
                def _():
                    up(a, dx, c).start()

                if c == 0:
                    @pl.when(has_prev)
                    def _():
                        down(a, dx).start()
        if c == 1:
            seg_copy.wait()
            masks()

    mrun[...] = jnp.full(mrun.shape, NEG, F32)
    lrun[...] = jnp.zeros(lrun.shape, F32)
    acc[...] = jnp.zeros(acc.shape, F32)

    for a in range(2):
        for dx in STEPS:
            @pl.when(has_prev)
            def _():
                up(a, dx, 1).wait_recv()

            @pl.when(has_both)
            def _():
                up2(a, dx).start()

    def k_tile(i):
        return kbuf[pl.ds(pl.multiple_of(i * B, B), B), :]

    def v_tile(i):
        return vbuf[pl.ds(pl.multiple_of(i * B, B), B), :]

    def forward(b, i):
        l = i - b
        n = b * TILES + l
        s = dot_nt(qst[b], k_tile(i)) * C2
        bias_t = bias[b, l]
        s = s + jnp.concatenate([bias_t, bias_t], axis=0)
        m_old = mrun[b]
        m_new = jnp.maximum(m_old, jnp.max(s, axis=1, keepdims=True))
        e = jnp.exp2(s - wide(m_new))
        alpha = jnp.exp2(m_old - m_new)
        mrun[b] = m_new
        mtile[n] = m_new
        lrun[b] = lrun[b] * alpha + jnp.sum(e, axis=1, keepdims=True)
        e16 = e.astype(BF16)
        pbuf[n] = e16
        acc[b] = acc[b] * alpha + dot_nn(e16, v_tile(i))

    def local(arrays):
        for a in arrays:
            for dx in STEPS:
                arrived(a, dx, 0)

                @pl.when(has_prev)
                def _():
                    down(a, dx).start()

    def here(a):
        for dx in STEPS:
            arrived(a, dx, 1)

    local((2, 3))
    here(2)
    here(3)

    def two(b, i):
        def step(n, carry):
            forward(b, i - n)
            return carry

        lax.fori_loop(0, 2, step, 0)

    two(0, 4)
    local((4, 5))

    @pl.when(has_prev)
    def _():
        for a in range(2):
            for dx in STEPS:
                up(a, dx, 0).wait_recv()

    two(0, 2)
    here(4)
    here(5)
    dkT[...] = jnp.zeros(dkT.shape, F32)
    dvT[...] = jnp.zeros(dvT.shape, F32)

    def turned(b):
        qT[b] = jnp.transpose(qst[b].astype(F32)).astype(BF16)
        gT[b] = jnp.transpose(gst[b].astype(F32)).astype(BF16)

    turned(0)

    def finish(b):
        linv = 1.0 / lrun[b]
        lrun[b] = linv
        o16 = (acc[b] * linv).astype(BF16)
        obuf[b] = o16
        d = jnp.sum(gst[b].astype(F32) * o16.astype(F32), axis=1, keepdims=True)
        delta[b] = jnp.broadcast_to(d, (2 * B, D))
        acc[b] = jnp.zeros((2 * B, D), F32)

    @pl.when(has_prev2)
    def _():
        for a in range(2):
            for dx in STEPS:
                up2(a, dx).wait_recv()

    forward(0, 0)
    finish(0)

    def out_src(a, c, x):
        if a < 4:
            ref = obuf if a < 2 else dqbuf
            return ref.at[2 - 2 * c, pl.ds(pl.multiple_of((a % 2) * B + x * PIECE, PIECE), PIECE), :]
        return fin.at[a - 4, c, pl.ds(pl.multiple_of(x * PIECE, PIECE), PIECE), :]

    def out_dst(a, head_of):
        if a < 4:
            ref = o_out if a < 2 else dq_out
            return ref.at[:, pl.ds(pl.multiple_of((2 * head_of + a % 2) * D, D), D)]
        ref = dk_out if a == 4 else dv_out
        return ref.at[:, pl.ds(pl.multiple_of(head_of * D, D), D)]

    def give(a, dx, c):
        x = (t + dx) % 4
        return pltpu.make_async_remote_copy(
            src_ref=out_src(a, c, x), dst_ref=out_dst(a, head),
            send_sem=out_send.at[a, dx, c], recv_sem=out_recv.at[a, dx, core],
            device_id=(chip * 2 + c, x), device_id_type=MESH)

    def given(a, dx, c):
        x = (t + 4 - dx) % 4
        return pltpu.make_async_remote_copy(
            src_ref=out_src(a, core, t), dst_ref=out_dst(a, 2 * x + c),
            send_sem=out_send.at[a, dx, c], recv_sem=out_recv.at[a, dx, c],
            device_id=(chip * 2 + c, x), device_id_type=MESH)

    def keep(a):
        return pltpu.make_async_copy(out_src(a, core, t), out_dst(a, head), out_own.at[a])

    def give_tile(a, c):
        for dx in (2, 1, 3):
            give(a, dx, c).start()

        @pl.when(core == c)
        def _():
            keep(a).start()

        @pl.when(core != c)
        def _():
            give(a, 0, c).start()

    def backward(b, i):
        n = b * TILES + i - b
        r = jnp.exp2(mtile[n] - mrun[b]) * lrun[b]
        prob = pbuf[n].astype(F32) * wide(r)
        dp = dot_nt(gst[b], v_tile(i))
        ds = (prob * (dp - wide(delta[b]))).astype(BF16)
        dvT[i] += dot_nn(gT[b], prob.astype(BF16))
        dkT[i] += dot_nn(qT[b], ds)
        acc[b] += dot_nn(ds, k_tile(i))

    def back(m, a):
        return hop(48 + 2 * m + a, snd.at[m, a], rcv.at[m, a], nxt if m == 3 else prv)

    def ahead(a):
        ref = obuf if a == 0 else dqbuf
        return hop(56 + a, ref.at[1], ref.at[2], nxt)

    def send_back(m, i, cond):
        for a, ref in ((0, dkT), (1, dvT)):
            snd[m, a] = ref[i].astype(BF16)

            @pl.when(cond)
            def _():
                back(m, a).start()

    backward(0, 0)
    send_back(0, 0, has_prev2)
    give_tile(0, 1)
    give_tile(1, 1)

    @pl.when(has_next)
    def _():
        for a in range(4):
            for dx in STEPS:
                down(a, dx).wait_recv()

    def late(n, carry):
        forward(1, 5 - n)
        return carry

    lax.fori_loop(0, TILES, late, 0)

    @pl.when(has_next)
    def _():
        for a in (4, 5):
            for dx in STEPS:
                down(a, dx).wait_recv()

    finish(1)

    @pl.when(has_next)
    def _():
        ahead(0).start()

    turned(1)
    backward(1, 5)
    send_back(3, 5, has_next)

    def both(n, carry):
        backward(n, 1)
        return carry

    lax.fori_loop(0, 2, both, 0)
    send_back(1, 1, has_prev)

    def rest(n, carry):
        backward(1, 2 + n)
        return carry

    lax.fori_loop(0, 3, rest, 0)
    dqbuf[1] = (acc[1] * SCALE).astype(BF16)

    @pl.when(has_next)
    def _():
        ahead(1).start()

    backward(0, 2)
    for a, ref in ((0, dkT), (1, dvT)):
        @pl.when(has_both)
        def _():
            back(0, a).wait_recv()
            snd[2, a] = (ref[2] + rcv[0, a].astype(F32)).astype(BF16)

        @pl.when(last)
        def _():
            snd[2, a] = ref[2].astype(BF16)

        @pl.when(has_prev)
        def _():
            back(2, a).start()

    def tail(n, carry):
        backward(0, 3 + n)
        return carry

    lax.fori_loop(0, 2, tail, 0)
    dqbuf[0] = (acc[0] * SCALE).astype(BF16)
    give_tile(2, 1)
    give_tile(3, 1)

    @pl.when(first)
    def _():
        forward(2, 3)
        finish(2)
        turned(2)
        backward(2, 3)
        dqbuf[2] = (acc[2] * SCALE).astype(BF16)

    @pl.when(has_prev)
    def _():
        ahead(0).wait_recv()

    give_tile(0, 0)
    give_tile(1, 0)
    for i in range(2):
        for a, ref in ((0, dkT), (1, dvT)):
            if i == 0:
                @pl.when(has_next)
                def _():
                    back(1, a).wait_recv()
                    ref[3] = ref[3] + rcv[1, a].astype(F32)

                @pl.when(has_prev)
                def _():
                    back(3, a).wait_recv()
                    ref[3] = ref[3] + rcv[3, a].astype(F32)
            else:
                @pl.when(has_next)
                def _():
                    back(2, a).wait_recv()
                    ref[4] = ref[4] + rcv[2, a].astype(F32)

            fin[a, i] = jnp.transpose(ref[3 + i] * (SCALE if a == 0 else 1.0)).astype(BF16)
            give_tile(4 + a, i)

    @pl.when(has_prev)
    def _():
        ahead(1).wait_recv()

    give_tile(2, 0)
    give_tile(3, 0)

    for a in range(6):
        for dx, c in ALL:
            exchange(a, dx, c).wait_send()
            give(a, dx, c).wait_send()
            given(a, dx, c).wait_recv()
        keep(a).wait()

    @pl.when(has_next)
    def _():
        for a in range(2):
            for dx in STEPS:
                for c in range(2):
                    up(a, dx, c).wait_send()
            back(3, a).wait_send()
            ahead(a).wait_send()

    @pl.when(has_both)
    def _():
        for a in range(2):
            for dx in STEPS:
                up2(a, dx).wait_send()

    @pl.when(has_prev)
    def _():
        for a in range(6):
            for dx in STEPS:
                down(a, dx).wait_send()
        for a in range(2):
            back(1, a).wait_send()
            back(2, a).wait_send()

    @pl.when(has_prev2)
    def _():
        for a in range(2):
            back(0, a).wait_send()


def write_kernel(*refs):
    sems = refs[-1]
    copies = [pltpu.make_async_copy(refs[i], refs[4 + i], sems.at[i]) for i in range(4)]
    for copy in copies:
        copy.start()
    for copy in copies:
        copy.wait()


def body(pipe, query, key, value, grad_out, segment_ids):
    seg = segment_ids.reshape(-1, D)
    anyspace = pl.BlockSpec(memory_space=pl.ANY)
    dma = pltpu.SemaphoreType.DMA
    hbm = pl.BlockSpec(memory_space=pltpu.HBM)
    shapes = tuple(jax.ShapeDtypeStruct(x.shape, BF16) for x in (query, query, key, value))
    results = pl.pallas_call(
        functools.partial(kernel, pipe),
        out_shape=shapes,
        in_specs=[hbm] * 5,
        out_specs=(anyspace,) * 4,
        scratch_shapes=[
            pltpu.VMEM(seg.shape, jnp.int32),
            pltpu.VMEM((3, 2 * B, D), BF16),
            pltpu.VMEM((3, 2 * B, D), BF16),
            pltpu.VMEM((6 * B, D), BF16),
            pltpu.VMEM((6 * B, D), BF16),
            pltpu.VMEM((3, TILES, B, B), F32),
            pltpu.VMEM((3 * TILES, 2 * B, B), BF16),
            pltpu.VMEM((3 * TILES, 2 * B, D), F32),
            pltpu.VMEM((3, 2 * B, D), F32),
            pltpu.VMEM((3, 2 * B, D), F32),
            pltpu.VMEM((3, 2 * B, D), F32),
            pltpu.VMEM((3, 2 * B, D), F32),
            pltpu.VMEM((3, D, 2 * B), BF16),
            pltpu.VMEM((3, D, 2 * B), BF16),
            pltpu.VMEM((6, D, B), F32),
            pltpu.VMEM((6, D, B), F32),
            pltpu.VMEM((3, 2 * B, D), BF16),
            pltpu.VMEM((3, 2 * B, D), BF16),
            pltpu.VMEM((4, 2, D, B), BF16),
            pltpu.VMEM((4, 2, D, B), BF16),
            pltpu.VMEM((2, 2, B, D), BF16),
            dma(()), dma((6, 4, 2)), dma((6, 4, 2)), dma((6,)),
            dma((58,)), dma((58,)),
            dma((6, 4, 2)), dma((6, 4, 2)), dma((6,)),
        ],
        compiler_params=pltpu.CompilerParams(
            collective_id=0, has_side_effects=True, vmem_limit_bytes=40 * 1024 * 1024),
    )(*[pltpu.with_memory_space_constraint(x, pltpu.HBM) for x in (query, key, value, grad_out, seg)])
    return pl.pallas_call(
        write_kernel,
        out_shape=shapes,
        in_specs=[pl.BlockSpec(memory_space=pltpu.VMEM)] * 4,
        out_specs=(hbm,) * 4,
        scratch_shapes=[dma((4,))],
    )(*[pltpu.with_memory_space_constraint(x, pltpu.VMEM) for x in results])


def solution(mesh):
    spec = P(("pipe", "tensor"), None)
    return jax.shard_map(
        functools.partial(body, mesh.shape["pipe"]),
        mesh=mesh,
        in_specs=(spec,) * 4 + (P(),),
        out_specs=(spec,) * 4,
        check_vma=False,
    )
```

```python
import functools
import math

import jax
import jax.numpy as jnp
from jax import lax
from jax.experimental import pallas as pl
from jax.experimental.pallas import tpu as pltpu
from jax.sharding import PartitionSpec as P

MESH = pl.DeviceIdType.MESH
D = 128
WINDOW = 1024
SCALE = 168.0 ** -0.5
C2 = SCALE * math.log2(math.e)
NEG = -1e30
F32 = jnp.float32
BF16 = jnp.bfloat16
B = 256
PIECE = 64
TILES = 5


def dot_nt(a, b):
    return lax.dot_general(a, b, (((1,), (1,)), ((), ())), preferred_element_type=F32)


def dot_nn(a, b):
    return jnp.dot(a, b, preferred_element_type=F32)


def wide(x):
    return jnp.concatenate([x, x], axis=1)


def kernel(pipe, q_ref, k_ref, v_ref, g_ref, seg_hbm, o_out, dq_out, dk_out, dv_out,
           seg_ref, qst, gst, kbuf, vbuf, bias, pbuf, mtile, mrun, lrun, acc, delta,
           qT, gT, dkT, dvT, obuf, dqbuf, snd, rcv, fin,
           seg_sem, in_send, in_recv, own_sem, hop_send, hop_recv,
           out_send, out_recv, out_own, ready):
    p = lax.axis_index("pipe")
    t = lax.axis_index("tensor")
    core = p % 2
    other = 1 - core
    chip = p // 2
    chips = pipe // 2
    nxt = ((p + 2) % pipe, t)
    prv = ((p + pipe - 2) % pipe, t)
    head = 2 * t + core
    has_prev, has_prev2, has_next = chip >= 1, chip >= 2, chip < chips - 1
    has_both = has_prev & has_next
    first, last = chip == 0, chip == chips - 1
    FAR = [(dx, c) for dx in (2, 1, 3) for c in range(2)]
    ALL = [(0, other)] + FAR

    seg_copy = pltpu.make_async_copy(seg_hbm, seg_ref, seg_sem)
    seg_copy.start()
    barrier = pltpu.get_barrier_semaphore()
    def greet(chip_of, c, x):
        pl.semaphore_signal(barrier, inc=1, device_id=(chip_of * 2 + c, x), device_id_type=MESH)

    origin = first & (core == 0) & (t == 0)
    near_origin = (first & jnp.logical_not(origin)) | ((chip == 1) & (core == 0))

    @pl.when(jnp.logical_not(origin))
    def _():
        for dx, c in ALL:
            greet(chip, c, (t + dx) % 4)

        @pl.when(has_next)
        def _():
            for x in range(4):
                greet(chip + 1, 0, x)

            @pl.when(core == 1)
            def _():
                greet(chip + 1, 1, t)

        @pl.when(has_prev)
        def _():
            @pl.when(core == 0)
            def _():
                for x in range(4):
                    for c in range(2):
                        greet(chip - 1, c, x)

            @pl.when(core == 1)
            def _():
                greet(chip - 1, 1, t)

    n_prev, n_next = jnp.minimum(chip, 1), jnp.minimum(chips - 1 - chip, 1)
    pl.semaphore_wait(barrier, 7 + n_next * (4 + core) + n_prev * (8 - 7 * core) - near_origin.astype(jnp.int32))

    @pl.when(origin)
    def _():
        for dx, c in ALL:
            pl.semaphore_signal(ready, inc=1, device_id=(c, dx % 4), device_id_type=MESH)
        for x in range(4):
            pl.semaphore_signal(ready, inc=1, device_id=(2, x), device_id_type=MESH)

    def src_of(a, head_of):
        if a == 0:
            return k_ref.at[:, pl.ds(pl.multiple_of(head_of * D, D), D)]
        if a == 1:
            return v_ref.at[:, pl.ds(pl.multiple_of(head_of * D, D), D)]
        h = a % 2
        ref = q_ref if a < 4 else g_ref
        return ref.at[:, pl.ds(pl.multiple_of((2 * head_of + h) * D, D), D)]

    def rows_at(ref, tile, x):
        return ref.at[pl.ds(pl.multiple_of(tile * B + x * PIECE, PIECE), PIECE), :]

    def heads_at(a, tile, x):
        ref = qst if a < 4 else gst
        return ref.at[tile, pl.ds(pl.multiple_of((a % 2) * B + x * PIECE, PIECE), PIECE), :]

    shift = (1 - core) * n_prev
    tile_to = (1 - core) * (2 - n_prev)

    def exchange(a, dx, c):
        x = (t + dx) % 4
        if a < 2:
            dst, mark, chip_to = rows_at(kbuf if a == 0 else vbuf, 3 + core, t), core, chip
        else:
            dst, mark, chip_to = heads_at(a, tile_to, t), tile_to, chip - shift
        return pltpu.make_async_remote_copy(
            src_ref=src_of(a, 2 * x + c), dst_ref=dst,
            send_sem=in_send.at[a, dx, c], recv_sem=in_recv.at[a, dx, mark],
            device_id=(chip_to * 2 + c, x), device_id_type=MESH)

    def exchanged(a, dx, mark):
        x = (t + 4 - dx) % 4
        if a < 2:
            dst = rows_at(kbuf if a == 0 else vbuf, 3 + mark, x)
        else:
            dst = heads_at(a, mark, x)
        return pltpu.make_async_remote_copy(
            src_ref=src_of(a, head), dst_ref=dst,
            send_sem=in_send.at[a, dx, 0], recv_sem=in_recv.at[a, dx, mark],
            device_id=nxt, device_id_type=MESH)

    def own(a):
        if a < 2:
            dst = rows_at(kbuf if a == 0 else vbuf, 3 + core, t)
        else:
            dst = heads_at(a, tile_to, t)
        return pltpu.make_async_copy(src_of(a, head), dst, own_sem.at[a])

    def hop(at, src, dst, dev):
        return pltpu.make_async_remote_copy(
            src_ref=src, dst_ref=dst, send_sem=hop_send.at[at], recv_sem=hop_recv.at[at],
            device_id=dev, device_id_type=MESH)

    def up(a, dx, c):
        ref, x = kbuf if a == 0 else vbuf, (t + 4 - dx) % 4
        return hop(a * 8 + dx * 2 + c, rows_at(ref, 3 + c, x), rows_at(ref, 1 + c, x), nxt)

    def up2(a, dx):
        ref, x = kbuf if a == 0 else vbuf, (t + 4 - dx) % 4
        return hop(16 + a * 4 + dx, rows_at(ref, 2, x), rows_at(ref, 0, x), nxt)

    def down(a, dx):
        ref, x = kbuf if a == 0 else vbuf, (t + 4 - dx) % 4
        return hop(24 + a * 4 + dx, rows_at(ref, 3, x), rows_at(ref, 5, x), prv)

    above_origin = (chip == 1) & (core == 0) & (t == 0)

    def to_origin(a, dx, c):
        chip_to = chip if a < 2 else chip - shift
        return (chip_to == 0) & ((t + dx) % 4 == 0) & (c == 0)

    for a in range(6):
        @pl.when(jnp.logical_not(to_origin(a, 0, other)))
        def _():
            exchange(a, 0, other).start()

        if a < 2:
            own(a).start()
        else:
            @pl.when(shift == 0)
            def _():
                own(a).start()

            @pl.when((shift == 1) & jnp.logical_not(to_origin(a, 0, core)))
            def _():
                exchange(a, 0, core).start()

    for a in range(6):
        for dx, c in FAR:
            if c == 0:
                @pl.when(jnp.logical_not(to_origin(a, dx, c)))
                def _():
                    exchange(a, dx, c).start()
            else:
                exchange(a, dx, c).start()

    def zero_tile(i):
        kbuf[i * B:(i + 1) * B, :] = jnp.zeros((B, D), BF16)
        vbuf[i * B:(i + 1) * B, :] = jnp.zeros((B, D), BF16)

    @pl.when(first)
    def _():
        zero_tile(1)
        zero_tile(2)

    @pl.when(chip <= 1)
    def _():
        zero_tile(0)

    @pl.when(last)
    def _():
        zero_tile(5)
        qst[1] = jnp.zeros((2 * B, D), BF16)
        gst[1] = jnp.zeros((2 * B, D), BF16)

    def arrived(a, dx, c):
        mark = c if a < 2 else 2 - 2 * c
        if dx == 0:
            @pl.when(core == c)
            def _():
                own(a).wait()

            @pl.when(core != c)
            def _():
                exchanged(a, 0, mark).wait_recv()
        else:
            exchanged(a, dx, mark).wait_recv()

    STEPS = (0, 1, 3, 2)

    def masks():
        row = lax.broadcasted_iota(jnp.int32, (B, D), 0)
        col = lax.broadcasted_iota(jnp.int32, (B, D), 1)

        def seg_row(at):
            inside = (at >= 0) & (at < 4 * chips)
            r = seg_ref[pl.ds(jnp.minimum(jnp.maximum(at, 0), 4 * chips - 1), 1), :]
            return jnp.where(inside, r, -1)

        def seg_col(at):
            parts = [jnp.transpose(jnp.broadcast_to(seg_row(at + k), (D, D))) for k in range(2)]
            return jnp.concatenate(parts, axis=0)

        def mask(b, l, at, offset, qseg):
            for part in range(2):
                kseg = jnp.broadcast_to(seg_row(at + part), (B, D))
                gap = row - col + (offset - part * D)
                ok = (kseg == qseg) & (gap >= 0) & (gap < WINDOW)
                bias[b, l, :, part * D:(part + 1) * D] = jnp.where(ok, 0.0, NEG)

        for b in range(2):
            qseg = seg_col(4 * chip + 2 + 2 * b)

            def mask_tile(l, carry):
                mask(b, l, 4 * chip - 6 + 2 * (b + l), 4 * B - l * B, qseg)
                return carry

            lax.fori_loop(0, TILES, mask_tile, 0)

        @pl.when(first)
        def _():
            mask(2, 1, 4 * chip, 0, seg_col(4 * chip))

    seg_copy.wait()
    masks()
    mrun[...] = jnp.full(mrun.shape, NEG, F32)
    lrun[...] = jnp.zeros(lrun.shape, F32)
    acc[...] = jnp.zeros(acc.shape, F32)
    dkT[...] = jnp.zeros(dkT.shape, F32)
    dvT[...] = jnp.zeros(dvT.shape, F32)

    for a in range(2):
        for dx in STEPS:
            arrived(a, dx, 1)

            @pl.when(has_next)
            def _():
                up(a, dx, 1).start()

    for a in range(2):
        for dx in STEPS:
            @pl.when(has_prev | (dx != t) | origin)
            def _():
                arrived(a, dx, 0)

                @pl.when(has_next)
                def _():
                    up(a, dx, 0).start()

                @pl.when(has_prev & jnp.logical_not(above_origin))
                def _():
                    down(a, dx).start()

    def arrived_first(a):
        exchanged(a, t, 0).wait_recv()

    @pl.when(near_origin)
    def _():
        pl.semaphore_wait(ready, 1)
        steps = (4 - t) % 4

        @pl.when(first)
        def _():
            for a in range(2):
                exchange(a, steps, 0).start()

        for a in range(2, 6):
            exchange(a, steps, 0).start()

        @pl.when(above_origin)
        def _():
            for a in range(2):
                for dx in STEPS:
                    down(a, dx).start()

    for a in range(2):
        for dx in STEPS:
            @pl.when(has_prev)
            def _():
                up(a, dx, 1).wait_recv()

            @pl.when(has_both)
            def _():
                up2(a, dx).start()

    def k_tile(i):
        return kbuf[pl.ds(pl.multiple_of(i * B, B), B), :]

    def v_tile(i):
        return vbuf[pl.ds(pl.multiple_of(i * B, B), B), :]

    def forward(b, i):
        l = i - b
        n = b * TILES + l
        s = dot_nt(qst[b], k_tile(i)) * C2
        bias_t = bias[b, l]
        s = s + jnp.concatenate([bias_t, bias_t], axis=0)
        m_old = mrun[b]
        m_new = jnp.maximum(m_old, jnp.max(s, axis=1, keepdims=True))
        e = jnp.exp2(s - wide(m_new))
        alpha = jnp.exp2(m_old - m_new)
        mrun[b] = m_new
        mtile[n] = m_new
        lrun[b] = lrun[b] * alpha + jnp.sum(e, axis=1, keepdims=True)
        e16 = e.astype(BF16)
        pbuf[n] = e16
        acc[b] = acc[b] * alpha + dot_nn(e16, v_tile(i))

    def here(a):
        for dx in STEPS:
            arrived(a, dx, 1)

    here(2)
    here(3)
    n_first = 1 - n_prev
    early_tile, late_tile = 3 - 2 * n_first, 1 + 2 * n_first

    def early(b, diagonal):
        def step(n, carry):
            forward(b, jnp.where(n < 2, diagonal - n, jnp.where(n == 2, early_tile, 2)) if b else
                    jnp.where(n == 0, 4, jnp.where(n == 1, early_tile, 2)))
            return carry

        lax.fori_loop(0, 4 if b else 3, step, 0)

    early(0, 4)
    here(4)
    here(5)

    def turned(b):
        qT[b] = jnp.transpose(qst[b].astype(F32)).astype(BF16)
        gT[b] = jnp.transpose(gst[b].astype(F32)).astype(BF16)

    turned(0)

    def finish(b):
        linv = 1.0 / lrun[b]
        lrun[b] = linv
        o16 = (acc[b] * linv).astype(BF16)
        obuf[b] = o16
        d = jnp.sum(gst[b].astype(F32) * o16.astype(F32), axis=1, keepdims=True)
        delta[b] = jnp.broadcast_to(d, (2 * B, D))
        acc[b] = jnp.zeros((2 * B, D), F32)

    def heads_out(a, tile, x):
        ref = obuf if a < 2 else dqbuf
        return ref.at[tile, pl.ds(pl.multiple_of((a % 2) * B + x * PIECE, PIECE), PIECE), :]

    def fin_at(a, c, x):
        return fin.at[a - 4, c, pl.ds(pl.multiple_of(x * PIECE, PIECE), PIECE), :]

    def out_dst(a, head_of):
        if a < 4:
            ref = o_out if a < 2 else dq_out
            return ref.at[:, pl.ds(pl.multiple_of((2 * head_of + a % 2) * D, D), D)]
        ref = dk_out if a == 4 else dv_out
        return ref.at[:, pl.ds(pl.multiple_of(head_of * D, D), D)]

    def give(a, dx, part):
        x = (t + dx) % 4
        if a < 4:
            src, dev = heads_out(a, part, x), ((chip + part % 2) * 2 + (1 if part == 0 else 0), x)
        else:
            src, dev = fin_at(a, part, x), (chip * 2 + part, x)
        return pltpu.make_async_remote_copy(
            src_ref=src, dst_ref=out_dst(a, head),
            send_sem=out_send.at[a, dx, part], recv_sem=out_recv.at[a, dx, core],
            device_id=dev, device_id_type=MESH)

    def given(a, dx, c):
        x = (t + 4 - dx) % 4
        return pltpu.make_async_remote_copy(
            src_ref=heads_out(a, 0, t) if a < 4 else fin_at(a, 0, t), dst_ref=out_dst(a, 2 * x + c),
            send_sem=out_send.at[a, dx, 0], recv_sem=out_recv.at[a, dx, c],
            device_id=nxt, device_id_type=MESH)

    def keep(a, part):
        src = heads_out(a, part, t) if a < 4 else fin_at(a, part, t)
        return pltpu.make_async_copy(src, out_dst(a, head), out_own.at[a])

    def give_tile(a, part):
        for dx in (2, 1, 3):
            give(a, dx, part).start()
        if a < 4 and part == 1:
            give(a, 0, part).start()
        else:
            c = part if a >= 4 else (1 if part == 0 else 0)

            @pl.when(core == c)
            def _():
                keep(a, part).start()

            @pl.when(core != c)
            def _():
                give(a, 0, part).start()

    def backward(b, i):
        n = b * TILES + i - b
        r = jnp.exp2(mtile[n] - mrun[b]) * lrun[b]
        prob = pbuf[n].astype(F32) * wide(r)
        dp = dot_nt(gst[b], v_tile(i))
        ds = (prob * (dp - wide(delta[b]))).astype(BF16)
        dvT[i] += dot_nn(gT[b], prob.astype(BF16))
        dkT[i] += dot_nn(qT[b], ds)
        acc[b] += dot_nn(ds, k_tile(i))

    def back(m, a):
        return hop(48 + 2 * m + a, snd.at[m, a], rcv.at[m, a], nxt if m == 3 else prv)

    def send_back(m, i, cond):
        for a, ref in ((0, dkT), (1, dvT)):
            snd[m, a] = ref[i].astype(BF16)

            @pl.when(cond)
            def _():
                back(m, a).start()

    def next_here(arrays):
        @pl.when(has_next)
        def _():
            for a in arrays:
                for dx in STEPS:
                    exchanged(a, dx, 1).wait_recv()

    @pl.when(has_next)
    def _():
        for a in range(2):
            for dx in STEPS:
                down(a, dx).wait_recv()

    next_here((2, 3))

    early(1, 5)

    @pl.when(has_prev)
    def _():
        for a in range(2):
            for dx in STEPS:
                up(a, dx, 0).wait_recv()

    @pl.when(first & jnp.logical_not(origin))
    def _():
        for a in range(2):
            arrived_first(a)

            @pl.when(has_next)
            def _():
                up(a, t, 0).start()

    forward(1, late_tile)
    next_here((4, 5))
    finish(1)

    @pl.when(has_next)
    def _():
        give_tile(0, 1)
        give_tile(1, 1)

    forward(0, late_tile)

    @pl.when(has_prev2)
    def _():
        for a in range(2):
            for dx in STEPS:
                up2(a, dx).wait_recv()

    forward(0, 0)
    finish(0)
    backward(0, 0)
    send_back(0, 0, has_prev2)
    give_tile(0, 0)
    give_tile(1, 0)

    @pl.when(first)
    def _():
        for a in (2, 3, 4, 5):
            for dx in STEPS:
                arrived(a, dx, 0)
        forward(2, 3)
        finish(2)
        turned(2)
        backward(2, 3)
        dqbuf[2] = (acc[2] * SCALE).astype(BF16)
        for a in range(4):
            give_tile(a, 2)

    turned(1)
    backward(1, 5)
    send_back(3, 5, has_next)

    def both(n, carry):
        backward(n, 1)
        return carry

    lax.fori_loop(0, 2, both, 0)
    send_back(1, 1, has_prev)

    def both2(n, carry):
        backward(n, 2)
        return carry

    lax.fori_loop(0, 2, both2, 0)
    backward(1, 3)
    for a, ref in ((0, dkT), (1, dvT)):
        @pl.when(has_both)
        def _():
            back(0, a).wait_recv()
            snd[2, a] = (ref[2] + rcv[0, a].astype(F32)).astype(BF16)

        @pl.when(last)
        def _():
            snd[2, a] = ref[2].astype(BF16)

        @pl.when(has_prev)
        def _():
            back(2, a).start()

    backward(1, 4)
    dqbuf[1] = (acc[1] * SCALE).astype(BF16)

    @pl.when(has_next)
    def _():
        give_tile(2, 1)
        give_tile(3, 1)

    def tail(n, carry):
        backward(0, 3 + n)
        return carry

    lax.fori_loop(0, 2, tail, 0)
    dqbuf[0] = (acc[0] * SCALE).astype(BF16)
    give_tile(2, 0)
    give_tile(3, 0)

    for i in range(2):
        for a, ref in ((0, dkT), (1, dvT)):
            if i == 0:
                @pl.when(has_next)
                def _():
                    back(1, a).wait_recv()
                    ref[3] = ref[3] + rcv[1, a].astype(F32)

                @pl.when(has_prev)
                def _():
                    back(3, a).wait_recv()
                    ref[3] = ref[3] + rcv[3, a].astype(F32)
            else:
                @pl.when(has_next)
                def _():
                    back(2, a).wait_recv()
                    ref[4] = ref[4] + rcv[2, a].astype(F32)

            fin[a, i] = jnp.transpose(ref[3 + i] * (SCALE if a == 0 else 1.0)).astype(BF16)
            give_tile(4 + a, i)

    for a in range(6):
        for dx, c in ALL:
            exchange(a, dx, c).wait_send()
        if a >= 2:
            @pl.when(shift == 1)
            def _():
                exchange(a, 0, core).wait_send()

    def sent(a, part, c):
        for dx in (1, 2, 3):
            give(a, dx, part).wait_send()

        @pl.when(core != c)
        def _():
            give(a, 0, part).wait_send()

    for a in range(6):
        for dx, c in ALL:
            given(a, dx, c).wait_recv()
        if a < 4:
            @pl.when(core == 1)
            def _():
                keep(a, 0).wait()

            @pl.when((core == 0) & has_prev)
            def _():
                given(a, 0, core).wait_recv()

            @pl.when((core == 0) & first)
            def _():
                keep(a, 2).wait()

            sent(a, 0, 1)

            @pl.when(has_next)
            def _():
                for dx in STEPS:
                    give(a, dx, 1).wait_send()

            @pl.when(first)
            def _():
                sent(a, 2, 0)
        else:
            keep(a, core).wait()
            for c in range(2):
                sent(a, c, c)

    @pl.when(has_next)
    def _():
        for a in range(2):
            for dx in STEPS:
                for c in range(2):
                    up(a, dx, c).wait_send()
            back(3, a).wait_send()

    @pl.when(has_both)
    def _():
        for a in range(2):
            for dx in STEPS:
                up2(a, dx).wait_send()

    @pl.when(has_prev)
    def _():
        for a in range(2):
            for dx in STEPS:
                down(a, dx).wait_send()
            back(1, a).wait_send()
            back(2, a).wait_send()

    @pl.when(has_prev2)
    def _():
        for a in range(2):
            back(0, a).wait_send()


def write_kernel(*refs):
    sems = refs[-1]
    copies = [pltpu.make_async_copy(refs[i], refs[4 + i], sems.at[i]) for i in range(4)]
    for copy in copies:
        copy.start()
    for copy in copies:
        copy.wait()


def body(pipe, query, key, value, grad_out, segment_ids):
    seg = segment_ids.reshape(-1, D)
    anyspace = pl.BlockSpec(memory_space=pl.ANY)
    dma = pltpu.SemaphoreType.DMA
    hbm = pl.BlockSpec(memory_space=pltpu.HBM)
    shapes = tuple(jax.ShapeDtypeStruct(x.shape, BF16) for x in (query, query, key, value))
    results = pl.pallas_call(
        functools.partial(kernel, pipe),
        out_shape=shapes,
        in_specs=[hbm] * 5,
        out_specs=(anyspace,) * 4,
        scratch_shapes=[
            pltpu.VMEM(seg.shape, jnp.int32),
            pltpu.VMEM((3, 2 * B, D), BF16),
            pltpu.VMEM((3, 2 * B, D), BF16),
            pltpu.VMEM((6 * B, D), BF16),
            pltpu.VMEM((6 * B, D), BF16),
            pltpu.VMEM((3, TILES, B, B), F32),
            pltpu.VMEM((3 * TILES, 2 * B, B), BF16),
            pltpu.VMEM((3 * TILES, 2 * B, D), F32),
            pltpu.VMEM((3, 2 * B, D), F32),
            pltpu.VMEM((3, 2 * B, D), F32),
            pltpu.VMEM((3, 2 * B, D), F32),
            pltpu.VMEM((3, 2 * B, D), F32),
            pltpu.VMEM((3, D, 2 * B), BF16),
            pltpu.VMEM((3, D, 2 * B), BF16),
            pltpu.VMEM((6, D, B), F32),
            pltpu.VMEM((6, D, B), F32),
            pltpu.VMEM((3, 2 * B, D), BF16),
            pltpu.VMEM((3, 2 * B, D), BF16),
            pltpu.VMEM((4, 2, D, B), BF16),
            pltpu.VMEM((4, 2, D, B), BF16),
            pltpu.VMEM((2, 2, B, D), BF16),
            dma(()), dma((6, 4, 3)), dma((6, 4, 3)), dma((6,)),
            dma((56,)), dma((56,)),
            dma((6, 4, 3)), dma((6, 4, 3)), dma((6,)), pltpu.SemaphoreType.REGULAR,
        ],
        compiler_params=pltpu.CompilerParams(
            collective_id=0, has_side_effects=True, vmem_limit_bytes=40 * 1024 * 1024),
    )(*[pltpu.with_memory_space_constraint(x, pltpu.HBM) for x in (query, key, value, grad_out, seg)])
    return pl.pallas_call(
        write_kernel,
        out_shape=shapes,
        in_specs=[pl.BlockSpec(memory_space=pltpu.VMEM)] * 4,
        out_specs=(hbm,) * 4,
        scratch_shapes=[dma((4,))],
    )(*[pltpu.with_memory_space_constraint(x, pltpu.VMEM) for x in results])


def solution(mesh):
    spec = P(("pipe", "tensor"), None)
    return jax.shard_map(
        functools.partial(body, mesh.shape["pipe"]),
        mesh=mesh,
        in_specs=(spec,) * 4 + (P(),),
        out_specs=(spec,) * 4,
        check_vma=False,
    )
```

```python
import functools
import math

import jax
import jax.numpy as jnp
from jax import lax
from jax.experimental import pallas as pl
from jax.experimental.pallas import tpu as pltpu
from jax.sharding import PartitionSpec as P

MESH = pl.DeviceIdType.MESH
D = 128
WINDOW = 1024
SCALE = 168.0 ** -0.5
C2 = SCALE * math.log2(math.e)
NEG = -1e30
F32 = jnp.float32
BF16 = jnp.bfloat16
B = 256
PIECE = 64
TILES = 5


def dot_nt(a, b):
    return lax.dot_general(a, b, (((1,), (1,)), ((), ())), preferred_element_type=F32)


def dot_nn(a, b):
    return jnp.dot(a, b, preferred_element_type=F32)


def wide(x):
    return jnp.concatenate([x, x], axis=1)


def kernel(pipe, q_ref, k_ref, v_ref, g_ref, seg_hbm, o_out, dq_out, dk_out, dv_out,
           seg_ref, qst, gst, kbuf, vbuf, bias, pbuf, mtile, mrun, lrun, acc, delta,
           qT, gT, dkT, dvT, obuf, dqbuf, snd, rcv, fin,
           seg_sem, in_send, in_recv, own_sem, hop_send, hop_recv,
           out_send, out_recv, out_own, ready):
    p = lax.axis_index("pipe")
    t = lax.axis_index("tensor")
    core = p % 2
    other = 1 - core
    chip = p // 2
    chips = pipe // 2
    nxt = ((p + 2) % pipe, t)
    prv = ((p + pipe - 2) % pipe, t)
    head = 2 * t + core
    has_prev, has_prev2, has_next = chip >= 1, chip >= 2, chip < chips - 1
    has_both = has_prev & has_next
    first, last = chip == 0, chip == chips - 1
    FAR = [(dx, c) for dx in (2, 1, 3) for c in range(2)]
    ALL = [(0, other)] + FAR

    seg_copy = pltpu.make_async_copy(seg_hbm, seg_ref, seg_sem)
    seg_copy.start()
    barrier = pltpu.get_barrier_semaphore()
    def greet(chip_of, c, x):
        pl.semaphore_signal(barrier, inc=1, device_id=(chip_of * 2 + c, x), device_id_type=MESH)

    origin = first & (core == 0) & (t == 0)
    near_origin = (first & jnp.logical_not(origin)) | ((chip == 1) & (core == 0))

    @pl.when(jnp.logical_not(origin))
    def _():
        for dx, c in ALL:
            greet(chip, c, (t + dx) % 4)

        @pl.when(has_next)
        def _():
            for x in range(4):
                greet(chip + 1, 0, x)

            @pl.when(core == 1)
            def _():
                greet(chip + 1, 1, t)

        @pl.when(has_prev)
        def _():
            @pl.when(core == 0)
            def _():
                for x in range(4):
                    for c in range(2):
                        greet(chip - 1, c, x)

            @pl.when(core == 1)
            def _():
                greet(chip - 1, 1, t)

    n_prev, n_next = jnp.minimum(chip, 1), jnp.minimum(chips - 1 - chip, 1)
    pl.semaphore_wait(barrier, 7 + n_next * (4 + core) + n_prev * (8 - 7 * core) - near_origin.astype(jnp.int32))

    @pl.when(origin)
    def _():
        for dx, c in ALL:
            pl.semaphore_signal(ready, inc=1, device_id=(c, dx % 4), device_id_type=MESH)
        for x in range(4):
            pl.semaphore_signal(ready, inc=1, device_id=(2, x), device_id_type=MESH)

    def src_of(a, head_of):
        if a == 0:
            return k_ref.at[:, pl.ds(pl.multiple_of(head_of * D, D), D)]
        if a == 1:
            return v_ref.at[:, pl.ds(pl.multiple_of(head_of * D, D), D)]
        h = a % 2
        ref = q_ref if a < 4 else g_ref
        return ref.at[:, pl.ds(pl.multiple_of((2 * head_of + h) * D, D), D)]

    def rows_at(ref, tile, x):
        return ref.at[pl.ds(pl.multiple_of(tile * B + x * PIECE, PIECE), PIECE), :]

    def heads_at(a, tile, x):
        ref = qst if a < 4 else gst
        return ref.at[tile, pl.ds(pl.multiple_of((a % 2) * B + x * PIECE, PIECE), PIECE), :]

    shift = (1 - core) * n_prev
    tile_to = (1 - core) * (2 - n_prev)

    def exchange(a, dx, c):
        x = (t + dx) % 4
        if a < 2:
            dst, mark, chip_to = rows_at(kbuf if a == 0 else vbuf, 3 + core, t), core, chip
        else:
            dst, mark, chip_to = heads_at(a, tile_to, t), tile_to, chip - shift
        return pltpu.make_async_remote_copy(
            src_ref=src_of(a, 2 * x + c), dst_ref=dst,
            send_sem=in_send.at[a, dx, c], recv_sem=in_recv.at[a, dx, mark],
            device_id=(chip_to * 2 + c, x), device_id_type=MESH)

    def exchanged(a, dx, mark):
        x = (t + 4 - dx) % 4
        if a < 2:
            dst = rows_at(kbuf if a == 0 else vbuf, 3 + mark, x)
        else:
            dst = heads_at(a, mark, x)
        return pltpu.make_async_remote_copy(
            src_ref=src_of(a, head), dst_ref=dst,
            send_sem=in_send.at[a, dx, 0], recv_sem=in_recv.at[a, dx, mark],
            device_id=nxt, device_id_type=MESH)

    def own(a):
        if a < 2:
            dst = rows_at(kbuf if a == 0 else vbuf, 3 + core, t)
        else:
            dst = heads_at(a, tile_to, t)
        return pltpu.make_async_copy(src_of(a, head), dst, own_sem.at[a])

    def hop(at, src, dst, dev):
        return pltpu.make_async_remote_copy(
            src_ref=src, dst_ref=dst, send_sem=hop_send.at[at], recv_sem=hop_recv.at[at],
            device_id=dev, device_id_type=MESH)

    def up(a, dx, c):
        ref, x = kbuf if a == 0 else vbuf, (t + 4 - dx) % 4
        return hop(a * 8 + dx * 2 + c, rows_at(ref, 3 + c, x), rows_at(ref, 1 + c, x), nxt)

    def up2(a, dx):
        ref, x = kbuf if a == 0 else vbuf, (t + 4 - dx) % 4
        return hop(16 + a * 4 + dx, rows_at(ref, 2, x), rows_at(ref, 0, x), nxt)

    def down(a, dx):
        ref, x = kbuf if a == 0 else vbuf, (t + 4 - dx) % 4
        return hop(24 + a * 4 + dx, rows_at(ref, 3, x), rows_at(ref, 5, x), prv)

    above_origin = (chip == 1) & (core == 0) & (t == 0)

    def to_origin(a, dx, c):
        chip_to = chip if a < 2 else chip - shift
        return (chip_to == 0) & ((t + dx) % 4 == 0) & (c == 0)

    for a in range(6):
        @pl.when(jnp.logical_not(to_origin(a, 0, other)))
        def _():
            exchange(a, 0, other).start()

        if a < 2:
            own(a).start()
        else:
            @pl.when(shift == 0)
            def _():
                own(a).start()

            @pl.when((shift == 1) & jnp.logical_not(to_origin(a, 0, core)))
            def _():
                exchange(a, 0, core).start()

    for a in range(6):
        for dx, c in FAR:
            if c == 0:
                @pl.when(jnp.logical_not(to_origin(a, dx, c)))
                def _():
                    exchange(a, dx, c).start()
            else:
                exchange(a, dx, c).start()

    def zero_tile(i):
        kbuf[i * B:(i + 1) * B, :] = jnp.zeros((B, D), BF16)
        vbuf[i * B:(i + 1) * B, :] = jnp.zeros((B, D), BF16)

    @pl.when(first)
    def _():
        zero_tile(1)
        zero_tile(2)

    @pl.when(chip <= 1)
    def _():
        zero_tile(0)

    @pl.when(last)
    def _():
        zero_tile(5)
        qst[1] = jnp.zeros((2 * B, D), BF16)
        gst[1] = jnp.zeros((2 * B, D), BF16)

    def arrived(a, dx, c):
        mark = c if a < 2 else 2 - 2 * c
        if dx == 0:
            @pl.when(core == c)
            def _():
                own(a).wait()

            @pl.when(core != c)
            def _():
                exchanged(a, 0, mark).wait_recv()
        else:
            exchanged(a, dx, mark).wait_recv()

    STEPS = (0, 1, 3, 2)

    def masks():
        row = lax.broadcasted_iota(jnp.int32, (B, D), 0)
        col = lax.broadcasted_iota(jnp.int32, (B, D), 1)

        def seg_row(at):
            inside = (at >= 0) & (at < 4 * chips)
            r = seg_ref[pl.ds(jnp.minimum(jnp.maximum(at, 0), 4 * chips - 1), 1), :]
            return jnp.where(inside, r, -1)

        def seg_col(at):
            parts = [jnp.transpose(jnp.broadcast_to(seg_row(at + k), (D, D))) for k in range(2)]
            return jnp.concatenate(parts, axis=0)

        def mask(b, l, at, offset, qseg):
            for part in range(2):
                kseg = jnp.broadcast_to(seg_row(at + part), (B, D))
                gap = row - col + (offset - part * D)
                ok = (kseg == qseg) & (gap >= 0) & (gap < WINDOW)
                bias[b, l, :, part * D:(part + 1) * D] = jnp.where(ok, 0.0, NEG)

        for b in range(2):
            qseg = seg_col(4 * chip + 2 + 2 * b)

            def mask_tile(l, carry):
                mask(b, l, 4 * chip - 6 + 2 * (b + l), 4 * B - l * B, qseg)
                return carry

            lax.fori_loop(0, TILES, mask_tile, 0)

        @pl.when(first)
        def _():
            mask(2, 1, 4 * chip, 0, seg_col(4 * chip))

    mrun[...] = jnp.full(mrun.shape, NEG, F32)
    lrun[...] = jnp.zeros(lrun.shape, F32)
    acc[...] = jnp.zeros(acc.shape, F32)
    dkT[...] = jnp.zeros(dkT.shape, F32)
    dvT[...] = jnp.zeros(dvT.shape, F32)

    for a in range(2):
        for dx in STEPS:
            arrived(a, dx, 1)

            @pl.when(has_next)
            def _():
                up(a, dx, 1).start()

    for a in range(2):
        for dx in STEPS:
            @pl.when(has_prev | (dx != t) | origin)
            def _():
                arrived(a, dx, 0)

                @pl.when(has_next)
                def _():
                    up(a, dx, 0).start()

                @pl.when(has_prev & jnp.logical_not(above_origin))
                def _():
                    down(a, dx).start()

    def arrived_first(a):
        exchanged(a, t, 0).wait_recv()

    @pl.when(near_origin)
    def _():
        pl.semaphore_wait(ready, 1)
        steps = (4 - t) % 4

        @pl.when(first)
        def _():
            for a in range(2):
                exchange(a, steps, 0).start()

        for a in range(2, 6):
            exchange(a, steps, 0).start()

        @pl.when(above_origin)
        def _():
            for a in range(2):
                for dx in STEPS:
                    down(a, dx).start()

    for a in range(2):
        for dx in STEPS:
            @pl.when(has_prev)
            def _():
                up(a, dx, 1).wait_recv()

            @pl.when(has_both)
            def _():
                up2(a, dx).start()

    def k_tile(i):
        return kbuf[pl.ds(pl.multiple_of(i * B, B), B), :]

    def v_tile(i):
        return vbuf[pl.ds(pl.multiple_of(i * B, B), B), :]

    def forward(b, i):
        l = i - b
        n = b * TILES + l
        s = dot_nt(qst[b], k_tile(i)) * C2
        bias_t = bias[b, l]
        s = s + jnp.concatenate([bias_t, bias_t], axis=0)
        m_old = mrun[b]
        m_new = jnp.maximum(m_old, jnp.max(s, axis=1, keepdims=True))
        e = jnp.exp2(s - wide(m_new))
        alpha = jnp.exp2(m_old - m_new)
        mrun[b] = m_new
        mtile[n] = m_new
        lrun[b] = lrun[b] * alpha + jnp.sum(e, axis=1, keepdims=True)
        e16 = e.astype(BF16)
        pbuf[n] = e16
        acc[b] = acc[b] * alpha + dot_nn(e16, v_tile(i))

    def here(a):
        for dx in STEPS:
            arrived(a, dx, 1)

    seg_copy.wait()
    masks()

    here(2)
    here(3)
    n_first = 1 - n_prev
    early_tile, late_tile = 3 - 2 * n_first, 1 + 2 * n_first

    def early(b, diagonal):
        def step(n, carry):
            forward(b, jnp.where(n < 2, diagonal - n, jnp.where(n == 2, early_tile, 2)) if b else
                    jnp.where(n == 0, 4, jnp.where(n == 1, early_tile, 2)))
            return carry

        lax.fori_loop(0, 4 if b else 3, step, 0)

    early(0, 4)
    here(4)
    here(5)

    def turned(b):
        qT[b] = jnp.transpose(qst[b].astype(F32)).astype(BF16)
        gT[b] = jnp.transpose(gst[b].astype(F32)).astype(BF16)

    turned(0)

    def finish(b):
        linv = 1.0 / lrun[b]
        lrun[b] = linv
        o16 = (acc[b] * linv).astype(BF16)
        obuf[b] = o16
        d = jnp.sum(gst[b].astype(F32) * o16.astype(F32), axis=1, keepdims=True)
        delta[b] = jnp.broadcast_to(d, (2 * B, D))
        acc[b] = jnp.zeros((2 * B, D), F32)

    def heads_out(a, tile, x):
        ref = obuf if a < 2 else dqbuf
        return ref.at[tile, pl.ds(pl.multiple_of((a % 2) * B + x * PIECE, PIECE), PIECE), :]

    def fin_at(a, c, x):
        return fin.at[a - 4, c, pl.ds(pl.multiple_of(x * PIECE, PIECE), PIECE), :]

    def out_dst(a, head_of):
        if a < 4:
            ref = o_out if a < 2 else dq_out
            return ref.at[:, pl.ds(pl.multiple_of((2 * head_of + a % 2) * D, D), D)]
        ref = dk_out if a == 4 else dv_out
        return ref.at[:, pl.ds(pl.multiple_of(head_of * D, D), D)]

    def give(a, dx, part):
        x = (t + dx) % 4
        if a < 4:
            src, dev = heads_out(a, part, x), ((chip + part % 2) * 2 + (1 if part == 0 else 0), x)
        else:
            src, dev = fin_at(a, part, x), (chip * 2 + part, x)
        return pltpu.make_async_remote_copy(
            src_ref=src, dst_ref=out_dst(a, head),
            send_sem=out_send.at[a, dx, part], recv_sem=out_recv.at[a, dx, core],
            device_id=dev, device_id_type=MESH)

    def given(a, dx, c):
        x = (t + 4 - dx) % 4
        return pltpu.make_async_remote_copy(
            src_ref=heads_out(a, 0, t) if a < 4 else fin_at(a, 0, t), dst_ref=out_dst(a, 2 * x + c),
            send_sem=out_send.at[a, dx, 0], recv_sem=out_recv.at[a, dx, c],
            device_id=nxt, device_id_type=MESH)

    def keep(a, part):
        src = heads_out(a, part, t) if a < 4 else fin_at(a, part, t)
        return pltpu.make_async_copy(src, out_dst(a, head), out_own.at[a])

    def give_tile(a, part):
        for dx in (2, 1, 3):
            give(a, dx, part).start()
        if a < 4 and part == 1:
            give(a, 0, part).start()
        else:
            c = part if a >= 4 else (1 if part == 0 else 0)

            @pl.when(core == c)
            def _():
                keep(a, part).start()

            @pl.when(core != c)
            def _():
                give(a, 0, part).start()

    def backward(b, i):
        n = b * TILES + i - b
        r = jnp.exp2(mtile[n] - mrun[b]) * lrun[b]
        prob = pbuf[n].astype(F32) * wide(r)
        dp = dot_nt(gst[b], v_tile(i))
        ds = (prob * (dp - wide(delta[b]))).astype(BF16)
        dvT[i] += dot_nn(gT[b], prob.astype(BF16))
        dkT[i] += dot_nn(qT[b], ds)
        acc[b] += dot_nn(ds, k_tile(i))

    def back(m, a):
        return hop(48 + 2 * m + a, snd.at[m, a], rcv.at[m, a], nxt if m == 3 else prv)

    def send_back(m, i, cond):
        for a, ref in ((0, dkT), (1, dvT)):
            snd[m, a] = ref[i].astype(BF16)

            @pl.when(cond)
            def _():
                back(m, a).start()

    def next_here(arrays):
        @pl.when(has_next)
        def _():
            for a in arrays:
                for dx in STEPS:
                    exchanged(a, dx, 1).wait_recv()

    @pl.when(has_next)
    def _():
        for a in range(2):
            for dx in STEPS:
                down(a, dx).wait_recv()

    next_here((2, 3))

    early(1, 5)

    @pl.when(has_prev)
    def _():
        for a in range(2):
            for dx in STEPS:
                up(a, dx, 0).wait_recv()

    @pl.when(first & jnp.logical_not(origin))
    def _():
        for a in range(2):
            arrived_first(a)

            @pl.when(has_next)
            def _():
                up(a, t, 0).start()

    forward(1, late_tile)
    next_here((4, 5))
    finish(1)

    @pl.when(has_next)
    def _():
        give_tile(0, 1)
        give_tile(1, 1)

    forward(0, late_tile)

    @pl.when(has_prev2)
    def _():
        for a in range(2):
            for dx in STEPS:
                up2(a, dx).wait_recv()

    forward(0, 0)
    finish(0)
    backward(0, 0)
    send_back(0, 0, has_prev2)
    give_tile(0, 0)
    give_tile(1, 0)

    @pl.when(first)
    def _():
        for a in (2, 3, 4, 5):
            for dx in STEPS:
                arrived(a, dx, 0)
        forward(2, 3)
        finish(2)
        turned(2)
        backward(2, 3)
        dqbuf[2] = (acc[2] * SCALE).astype(BF16)
        for a in range(4):
            give_tile(a, 2)

    turned(1)
    backward(1, 5)
    send_back(3, 5, has_next)

    def both(n, carry):
        backward(n, 1)
        return carry

    lax.fori_loop(0, 2, both, 0)
    send_back(1, 1, has_prev)

    def both2(n, carry):
        backward(n, 2)
        return carry

    lax.fori_loop(0, 2, both2, 0)
    backward(1, 3)
    backward(1, 4)
    dqbuf[1] = (acc[1] * SCALE).astype(BF16)

    @pl.when(has_next)
    def _():
        give_tile(2, 1)
        give_tile(3, 1)

    for a, ref in ((0, dkT), (1, dvT)):
        @pl.when(has_both)
        def _():
            back(0, a).wait_recv()
            snd[2, a] = (ref[2] + rcv[0, a].astype(F32)).astype(BF16)

        @pl.when(last)
        def _():
            snd[2, a] = ref[2].astype(BF16)

        @pl.when(has_prev)
        def _():
            back(2, a).start()

    def tail(n, carry):
        backward(0, 3 + n)
        return carry

    lax.fori_loop(0, 2, tail, 0)
    dqbuf[0] = (acc[0] * SCALE).astype(BF16)
    give_tile(2, 0)
    give_tile(3, 0)

    for i in range(2):
        for a, ref in ((0, dkT), (1, dvT)):
            if i == 0:
                @pl.when(has_next)
                def _():
                    back(1, a).wait_recv()
                    ref[3] = ref[3] + rcv[1, a].astype(F32)

                @pl.when(has_prev)
                def _():
                    back(3, a).wait_recv()
                    ref[3] = ref[3] + rcv[3, a].astype(F32)
            else:
                @pl.when(has_next)
                def _():
                    back(2, a).wait_recv()
                    ref[4] = ref[4] + rcv[2, a].astype(F32)

            fin[a, i] = jnp.transpose(ref[3 + i] * (SCALE if a == 0 else 1.0)).astype(BF16)
            give_tile(4 + a, i)

    for a in range(6):
        for dx, c in ALL:
            exchange(a, dx, c).wait_send()
        if a >= 2:
            @pl.when(shift == 1)
            def _():
                exchange(a, 0, core).wait_send()

    def sent(a, part, c):
        for dx in (1, 2, 3):
            give(a, dx, part).wait_send()

        @pl.when(core != c)
        def _():
            give(a, 0, part).wait_send()

    for a in range(6):
        for dx, c in ALL:
            given(a, dx, c).wait_recv()
        if a < 4:
            @pl.when(core == 1)
            def _():
                keep(a, 0).wait()

            @pl.when((core == 0) & has_prev)
            def _():
                given(a, 0, core).wait_recv()

            @pl.when((core == 0) & first)
            def _():
                keep(a, 2).wait()

            sent(a, 0, 1)

            @pl.when(has_next)
            def _():
                for dx in STEPS:
                    give(a, dx, 1).wait_send()

            @pl.when(first)
            def _():
                sent(a, 2, 0)
        else:
            keep(a, core).wait()
            for c in range(2):
                sent(a, c, c)

    @pl.when(has_next)
    def _():
        for a in range(2):
            for dx in STEPS:
                for c in range(2):
                    up(a, dx, c).wait_send()
            back(3, a).wait_send()

    @pl.when(has_both)
    def _():
        for a in range(2):
            for dx in STEPS:
                up2(a, dx).wait_send()

    @pl.when(has_prev)
    def _():
        for a in range(2):
            for dx in STEPS:
                down(a, dx).wait_send()
            back(1, a).wait_send()
            back(2, a).wait_send()

    @pl.when(has_prev2)
    def _():
        for a in range(2):
            back(0, a).wait_send()


def write_kernel(*refs):
    sems = refs[-1]
    copies = [pltpu.make_async_copy(refs[i], refs[4 + i], sems.at[i]) for i in range(4)]
    for copy in copies:
        copy.start()
    for copy in copies:
        copy.wait()


def body(pipe, query, key, value, grad_out, segment_ids):
    seg = segment_ids.reshape(-1, D)
    anyspace = pl.BlockSpec(memory_space=pl.ANY)
    dma = pltpu.SemaphoreType.DMA
    hbm = pl.BlockSpec(memory_space=pltpu.HBM)
    shapes = tuple(jax.ShapeDtypeStruct(x.shape, BF16) for x in (query, query, key, value))
    results = pl.pallas_call(
        functools.partial(kernel, pipe),
        out_shape=shapes,
        in_specs=[hbm] * 5,
        out_specs=(anyspace,) * 4,
        scratch_shapes=[
            pltpu.VMEM(seg.shape, jnp.int32),
            pltpu.VMEM((3, 2 * B, D), BF16),
            pltpu.VMEM((3, 2 * B, D), BF16),
            pltpu.VMEM((6 * B, D), BF16),
            pltpu.VMEM((6 * B, D), BF16),
            pltpu.VMEM((3, TILES, B, B), F32),
            pltpu.VMEM((3 * TILES, 2 * B, B), BF16),
            pltpu.VMEM((3 * TILES, 2 * B, D), F32),
            pltpu.VMEM((3, 2 * B, D), F32),
            pltpu.VMEM((3, 2 * B, D), F32),
            pltpu.VMEM((3, 2 * B, D), F32),
            pltpu.VMEM((3, 2 * B, D), F32),
            pltpu.VMEM((3, D, 2 * B), BF16),
            pltpu.VMEM((3, D, 2 * B), BF16),
            pltpu.VMEM((6, D, B), F32),
            pltpu.VMEM((6, D, B), F32),
            pltpu.VMEM((3, 2 * B, D), BF16),
            pltpu.VMEM((3, 2 * B, D), BF16),
            pltpu.VMEM((4, 2, D, B), BF16),
            pltpu.VMEM((4, 2, D, B), BF16),
            pltpu.VMEM((2, 2, B, D), BF16),
            dma(()), dma((6, 4, 3)), dma((6, 4, 3)), dma((6,)),
            dma((56,)), dma((56,)),
            dma((6, 4, 3)), dma((6, 4, 3)), dma((6,)), pltpu.SemaphoreType.REGULAR,
        ],
        compiler_params=pltpu.CompilerParams(
            collective_id=0, has_side_effects=True, vmem_limit_bytes=40 * 1024 * 1024),
    )(*[pltpu.with_memory_space_constraint(x, pltpu.HBM) for x in (query, key, value, grad_out, seg)])
    return pl.pallas_call(
        write_kernel,
        out_shape=shapes,
        in_specs=[pl.BlockSpec(memory_space=pltpu.VMEM)] * 4,
        out_specs=(hbm,) * 4,
        scratch_shapes=[dma((4,))],
    )(*[pltpu.with_memory_space_constraint(x, pltpu.VMEM) for x in results])


def solution(mesh):
    spec = P(("pipe", "tensor"), None)
    return jax.shard_map(
        functools.partial(body, mesh.shape["pipe"]),
        mesh=mesh,
        in_specs=(spec,) * 4 + (P(),),
        out_specs=(spec,) * 4,
        check_vma=False,
    )
```

```python
import functools
import math

import jax
import jax.numpy as jnp
from jax import lax
from jax.experimental import pallas as pl
from jax.experimental.pallas import tpu as pltpu
from jax.sharding import PartitionSpec as P

MESH = pl.DeviceIdType.MESH
D = 128
WINDOW = 1024
SCALE = 168.0 ** -0.5
C2 = SCALE * math.log2(math.e)
NEG = -1e30
F32 = jnp.float32
BF16 = jnp.bfloat16
B = 256
PIECE = 64
TILES = 5


def dot_nt(a, b):
    return lax.dot_general(a, b, (((1,), (1,)), ((), ())), preferred_element_type=F32)


def dot_nn(a, b):
    return jnp.dot(a, b, preferred_element_type=F32)


def wide(x):
    return jnp.concatenate([x, x], axis=1)


def kernel(pipe, q_ref, k_ref, v_ref, g_ref, seg_hbm, o_out, dq_out, dk_out, dv_out,
           seg_ref, qst, gst, kbuf, vbuf, bias, pbuf, mtile, mrun, lrun, acc, delta,
           qT, gT, dkT, dvT, obuf, dqbuf, snd, rcv, fin,
           seg_sem, in_send, in_recv, own_sem, hop_send, hop_recv,
           out_send, out_recv, out_own, ready):
    p = lax.axis_index("pipe")
    t = lax.axis_index("tensor")
    core = p % 2
    other = 1 - core
    chip = p // 2
    chips = pipe // 2
    nxt = ((p + 2) % pipe, t)
    prv = ((p + pipe - 2) % pipe, t)
    head = 2 * t + core
    has_prev, has_prev2, has_next = chip >= 1, chip >= 2, chip < chips - 1
    has_both = has_prev & has_next
    first, last = chip == 0, chip == chips - 1
    FAR = [(dx, c) for dx in (2, 1, 3) for c in range(2)]
    ALL = [(0, other)] + FAR

    seg_copy = pltpu.make_async_copy(seg_hbm, seg_ref, seg_sem)
    seg_copy.start()
    barrier = pltpu.get_barrier_semaphore()
    def greet(chip_of, c, x):
        pl.semaphore_signal(barrier, inc=1, device_id=(chip_of * 2 + c, x), device_id_type=MESH)

    origin = first & (core == 0) & (t == 0)
    near_origin = (first & jnp.logical_not(origin)) | ((chip == 1) & (core == 0))

    @pl.when(jnp.logical_not(origin))
    def _():
        for dx, c in ALL:
            greet(chip, c, (t + dx) % 4)

        @pl.when(has_next)
        def _():
            for x in range(4):
                greet(chip + 1, 0, x)

            @pl.when(core == 1)
            def _():
                greet(chip + 1, 1, t)

        @pl.when(has_prev)
        def _():
            @pl.when(core == 0)
            def _():
                for x in range(4):
                    for c in range(2):
                        greet(chip - 1, c, x)

            @pl.when(core == 1)
            def _():
                greet(chip - 1, 1, t)

    n_prev, n_next = jnp.minimum(chip, 1), jnp.minimum(chips - 1 - chip, 1)
    pl.semaphore_wait(barrier, 7 + n_next * (4 + core) + n_prev * (8 - 7 * core) - near_origin.astype(jnp.int32))

    @pl.when(origin)
    def _():
        for dx, c in ALL:
            pl.semaphore_signal(ready, inc=1, device_id=(c, dx % 4), device_id_type=MESH)
        for x in range(4):
            pl.semaphore_signal(ready, inc=1, device_id=(2, x), device_id_type=MESH)

    def src_of(a, head_of):
        if a == 0:
            return k_ref.at[:, pl.ds(pl.multiple_of(head_of * D, D), D)]
        if a == 1:
            return v_ref.at[:, pl.ds(pl.multiple_of(head_of * D, D), D)]
        h = a % 2
        ref = q_ref if a < 4 else g_ref
        return ref.at[:, pl.ds(pl.multiple_of((2 * head_of + h) * D, D), D)]

    def rows_at(ref, tile, x):
        return ref.at[pl.ds(pl.multiple_of(tile * B + x * PIECE, PIECE), PIECE), :]

    def heads_at(a, tile, x):
        ref = qst if a < 4 else gst
        return ref.at[tile, pl.ds(pl.multiple_of((a % 2) * B + x * PIECE, PIECE), PIECE), :]

    shift = (1 - core) * n_prev
    tile_to = (1 - core) * (2 - n_prev)

    def exchange(a, dx, c):
        x = (t + dx) % 4
        if a < 2:
            dst, mark, chip_to = rows_at(kbuf if a == 0 else vbuf, 3 + core, t), core, chip
        else:
            dst, mark, chip_to = heads_at(a, tile_to, t), tile_to, chip - shift
        return pltpu.make_async_remote_copy(
            src_ref=src_of(a, 2 * x + c), dst_ref=dst,
            send_sem=in_send.at[a, dx, c], recv_sem=in_recv.at[a, dx, mark],
            device_id=(chip_to * 2 + c, x), device_id_type=MESH)

    def exchanged(a, dx, mark):
        x = (t + 4 - dx) % 4
        if a < 2:
            dst = rows_at(kbuf if a == 0 else vbuf, 3 + mark, x)
        else:
            dst = heads_at(a, mark, x)
        return pltpu.make_async_remote_copy(
            src_ref=src_of(a, head), dst_ref=dst,
            send_sem=in_send.at[a, dx, 0], recv_sem=in_recv.at[a, dx, mark],
            device_id=nxt, device_id_type=MESH)

    def own(a):
        if a < 2:
            dst = rows_at(kbuf if a == 0 else vbuf, 3 + core, t)
        else:
            dst = heads_at(a, tile_to, t)
        return pltpu.make_async_copy(src_of(a, head), dst, own_sem.at[a])

    def hop(at, src, dst, dev):
        return pltpu.make_async_remote_copy(
            src_ref=src, dst_ref=dst, send_sem=hop_send.at[at], recv_sem=hop_recv.at[at],
            device_id=dev, device_id_type=MESH)

    def up(a, dx, c):
        ref, x = kbuf if a == 0 else vbuf, (t + 4 - dx) % 4
        return hop(a * 8 + dx * 2 + c, rows_at(ref, 3 + c, x), rows_at(ref, 1 + c, x), nxt)

    def up2(a, dx):
        ref, x = kbuf if a == 0 else vbuf, (t + 4 - dx) % 4
        return hop(16 + a * 4 + dx, rows_at(ref, 2, x), rows_at(ref, 0, x), nxt)

    def down(a, dx):
        ref, x = kbuf if a == 0 else vbuf, (t + 4 - dx) % 4
        return hop(24 + a * 4 + dx, rows_at(ref, 3, x), rows_at(ref, 5, x), prv)

    above_origin = (chip == 1) & (core == 0) & (t == 0)

    def to_origin(a, dx, c):
        chip_to = chip if a < 2 else chip - shift
        return (chip_to == 0) & ((t + dx) % 4 == 0) & (c == 0)

    for a in range(6):
        @pl.when(jnp.logical_not(to_origin(a, 0, other)))
        def _():
            exchange(a, 0, other).start()

        if a < 2:
            own(a).start()
        else:
            @pl.when(shift == 0)
            def _():
                own(a).start()

            @pl.when((shift == 1) & jnp.logical_not(to_origin(a, 0, core)))
            def _():
                exchange(a, 0, core).start()

    for a in range(6):
        for dx, c in FAR:
            if c == 0:
                @pl.when(jnp.logical_not(to_origin(a, dx, c)))
                def _():
                    exchange(a, dx, c).start()
            else:
                exchange(a, dx, c).start()

    def zero_tile(i):
        kbuf[i * B:(i + 1) * B, :] = jnp.zeros((B, D), BF16)
        vbuf[i * B:(i + 1) * B, :] = jnp.zeros((B, D), BF16)

    @pl.when(first)
    def _():
        zero_tile(1)
        zero_tile(2)

    @pl.when(chip <= 1)
    def _():
        zero_tile(0)

    @pl.when(last)
    def _():
        zero_tile(5)
        qst[1] = jnp.zeros((2 * B, D), BF16)
        gst[1] = jnp.zeros((2 * B, D), BF16)

    def arrived(a, dx, c):
        mark = c if a < 2 else 2 - 2 * c
        if dx == 0:
            @pl.when(core == c)
            def _():
                own(a).wait()

            @pl.when(core != c)
            def _():
                exchanged(a, 0, mark).wait_recv()
        else:
            exchanged(a, dx, mark).wait_recv()

    STEPS = (0, 1, 3, 2)

    def masks():
        row = lax.broadcasted_iota(jnp.int32, (B, D), 0)
        col = lax.broadcasted_iota(jnp.int32, (B, D), 1)

        def seg_row(at):
            inside = (at >= 0) & (at < 4 * chips)
            r = seg_ref[pl.ds(jnp.minimum(jnp.maximum(at, 0), 4 * chips - 1), 1), :]
            return jnp.where(inside, r, -1)

        def seg_col(at):
            parts = [jnp.transpose(jnp.broadcast_to(seg_row(at + k), (D, D))) for k in range(2)]
            return jnp.concatenate(parts, axis=0)

        def mask(b, l, at, offset, qseg):
            for part in range(2):
                kseg = jnp.broadcast_to(seg_row(at + part), (B, D))
                gap = row - col + (offset - part * D)
                ok = (kseg == qseg) & (gap >= 0) & (gap < WINDOW)
                bias[b, l, :, part * D:(part + 1) * D] = jnp.where(ok, 0.0, NEG)

        for b in range(2):
            qseg = seg_col(4 * chip + 2 + 2 * b)

            def mask_tile(l, carry):
                mask(b, l, 4 * chip - 6 + 2 * (b + l), 4 * B - l * B, qseg)
                return carry

            lax.fori_loop(0, TILES, mask_tile, 0)

        @pl.when(first)
        def _():
            mask(2, 1, 4 * chip, 0, seg_col(4 * chip))

    mrun[...] = jnp.full(mrun.shape, NEG, F32)
    lrun[...] = jnp.zeros(lrun.shape, F32)
    acc[...] = jnp.zeros(acc.shape, F32)
    dkT[...] = jnp.zeros(dkT.shape, F32)
    dvT[...] = jnp.zeros(dvT.shape, F32)

    for a in range(2):
        for dx in STEPS:
            arrived(a, dx, 1)

            @pl.when(has_next)
            def _():
                up(a, dx, 1).start()

    for a in range(2):
        for dx in STEPS:
            @pl.when(has_prev | (dx != t) | origin)
            def _():
                arrived(a, dx, 0)

                @pl.when(has_next)
                def _():
                    up(a, dx, 0).start()

                @pl.when(has_prev & jnp.logical_not(above_origin))
                def _():
                    down(a, dx).start()

    def arrived_first(a):
        exchanged(a, t, 0).wait_recv()

    @pl.when(near_origin)
    def _():
        pl.semaphore_wait(ready, 1)
        steps = (4 - t) % 4

        @pl.when(first)
        def _():
            for a in range(2):
                exchange(a, steps, 0).start()

        for a in range(2, 6):
            exchange(a, steps, 0).start()

        @pl.when(above_origin)
        def _():
            for a in range(2):
                for dx in STEPS:
                    down(a, dx).start()

    for a in range(2):
        for dx in STEPS:
            @pl.when(has_prev)
            def _():
                up(a, dx, 1).wait_recv()

            @pl.when(has_both)
            def _():
                up2(a, dx).start()

    def k_tile(i):
        return kbuf[pl.ds(pl.multiple_of(i * B, B), B), :]

    def v_tile(i):
        return vbuf[pl.ds(pl.multiple_of(i * B, B), B), :]

    def forward(b, i):
        l = i - b
        n = b * TILES + l
        s = dot_nt(qst[b], k_tile(i)) * C2
        bias_t = bias[b, l]
        s = s + jnp.concatenate([bias_t, bias_t], axis=0)
        m_old = mrun[b]
        m_new = jnp.maximum(m_old, jnp.max(s, axis=1, keepdims=True))
        e = jnp.exp2(s - wide(m_new))
        alpha = jnp.exp2(m_old - m_new)
        mrun[b] = m_new
        mtile[n] = m_new
        lrun[b] = lrun[b] * alpha + jnp.sum(e, axis=1, keepdims=True)
        e16 = e.astype(BF16)
        pbuf[n] = e16
        acc[b] = acc[b] * alpha + dot_nn(e16, v_tile(i))

    def here(a):
        for dx in STEPS:
            arrived(a, dx, 1)

    seg_copy.wait()
    masks()

    here(2)
    here(3)
    n_first = 1 - n_prev
    early_tile, late_tile = 3 - 2 * n_first, 1 + 2 * n_first

    def early(b, diagonal):
        def step(n, carry):
            forward(b, jnp.where(n < 2, diagonal - n, jnp.where(n == 2, early_tile, 2)) if b else
                    jnp.where(n == 0, 4, jnp.where(n == 1, early_tile, 2)))
            return carry

        lax.fori_loop(0, 4 if b else 3, step, 0)

    early(0, 4)
    here(4)
    here(5)

    def turned(b):
        qT[b] = jnp.transpose(qst[b].astype(F32)).astype(BF16)
        gT[b] = jnp.transpose(gst[b].astype(F32)).astype(BF16)

    turned(0)

    def finish(b):
        linv = 1.0 / lrun[b]
        lrun[b] = linv
        o16 = (acc[b] * linv).astype(BF16)
        obuf[b] = o16
        d = jnp.sum(gst[b].astype(F32) * o16.astype(F32), axis=1, keepdims=True)
        delta[b] = jnp.broadcast_to(d, (2 * B, D))
        acc[b] = jnp.zeros((2 * B, D), F32)

    def heads_out(a, tile, x):
        ref = obuf if a < 2 else dqbuf
        return ref.at[tile, pl.ds(pl.multiple_of((a % 2) * B + x * PIECE, PIECE), PIECE), :]

    def fin_at(a, c, x):
        return fin.at[a - 4, c, pl.ds(pl.multiple_of(x * PIECE, PIECE), PIECE), :]

    def out_dst(a, head_of):
        if a < 4:
            ref = o_out if a < 2 else dq_out
            return ref.at[:, pl.ds(pl.multiple_of((2 * head_of + a % 2) * D, D), D)]
        ref = dk_out if a == 4 else dv_out
        return ref.at[:, pl.ds(pl.multiple_of(head_of * D, D), D)]

    def give(a, dx, part):
        x = (t + dx) % 4
        if a < 4:
            src, dev = heads_out(a, part, x), ((chip + part % 2) * 2 + (1 if part == 0 else 0), x)
        else:
            src, dev = fin_at(a, part, x), (chip * 2 + part, x)
        return pltpu.make_async_remote_copy(
            src_ref=src, dst_ref=out_dst(a, head),
            send_sem=out_send.at[a, dx, part], recv_sem=out_recv.at[a, dx, core],
            device_id=dev, device_id_type=MESH)

    def given(a, dx, c):
        x = (t + 4 - dx) % 4
        return pltpu.make_async_remote_copy(
            src_ref=heads_out(a, 0, t) if a < 4 else fin_at(a, 0, t), dst_ref=out_dst(a, 2 * x + c),
            send_sem=out_send.at[a, dx, 0], recv_sem=out_recv.at[a, dx, c],
            device_id=nxt, device_id_type=MESH)

    def keep(a, part):
        src = heads_out(a, part, t) if a < 4 else fin_at(a, part, t)
        return pltpu.make_async_copy(src, out_dst(a, head), out_own.at[a])

    def give_tile(a, part):
        for dx in (2, 1, 3):
            give(a, dx, part).start()
        if a < 4 and part == 1:
            give(a, 0, part).start()
        else:
            c = part if a >= 4 else (1 if part == 0 else 0)

            @pl.when(core == c)
            def _():
                keep(a, part).start()

            @pl.when(core != c)
            def _():
                give(a, 0, part).start()

    def backward(b, i):
        n = b * TILES + i - b
        r = jnp.exp2(mtile[n] - mrun[b]) * lrun[b]
        prob = pbuf[n].astype(F32) * wide(r)
        dp = dot_nt(gst[b], v_tile(i))
        ds = (prob * (dp - wide(delta[b]))).astype(BF16)
        dvT[i] += dot_nn(gT[b], prob.astype(BF16))
        dkT[i] += dot_nn(qT[b], ds)
        acc[b] += dot_nn(ds, k_tile(i))

    def back(m, a, half):
        rows = pl.ds(half * 64, 64)
        return hop(48 + 4 * m + 2 * a + half, snd.at[m, a, rows], rcv.at[m, a, rows], nxt if m == 3 else prv)

    def returned(m, a):
        for half in range(2):
            back(m, a, half).wait_recv()

    def send_back(m, i, cond):
        for a, ref in ((0, dkT), (1, dvT)):
            snd[m, a] = ref[i].astype(BF16)

            @pl.when(cond)
            def _():
                for half in range(2):
                    back(m, a, half).start()

    def next_here(arrays):
        @pl.when(has_next)
        def _():
            for a in arrays:
                for dx in STEPS:
                    exchanged(a, dx, 1).wait_recv()

    @pl.when(has_next)
    def _():
        for a in range(2):
            for dx in STEPS:
                down(a, dx).wait_recv()

    next_here((2, 3))

    early(1, 5)

    @pl.when(has_prev)
    def _():
        for a in range(2):
            for dx in STEPS:
                up(a, dx, 0).wait_recv()

    @pl.when(first & jnp.logical_not(origin))
    def _():
        for a in range(2):
            arrived_first(a)

            @pl.when(has_next)
            def _():
                up(a, t, 0).start()

    forward(1, late_tile)
    next_here((4, 5))
    finish(1)

    @pl.when(has_next)
    def _():
        give_tile(0, 1)
        give_tile(1, 1)

    forward(0, late_tile)

    @pl.when(has_prev2)
    def _():
        for a in range(2):
            for dx in STEPS:
                up2(a, dx).wait_recv()

    forward(0, 0)
    finish(0)
    backward(0, 0)
    send_back(0, 0, has_prev2)
    give_tile(0, 0)
    give_tile(1, 0)

    @pl.when(first)
    def _():
        for a in (2, 3, 4, 5):
            for dx in STEPS:
                arrived(a, dx, 0)
        forward(2, 3)
        finish(2)
        turned(2)
        backward(2, 3)
        dqbuf[2] = (acc[2] * SCALE).astype(BF16)
        for a in range(4):
            give_tile(a, 2)

    turned(1)
    backward(1, 5)
    send_back(3, 5, has_next)

    def both(n, carry):
        backward(n, 1)
        return carry

    lax.fori_loop(0, 2, both, 0)
    send_back(1, 1, has_prev)

    def both2(n, carry):
        backward(n, 2)
        return carry

    lax.fori_loop(0, 2, both2, 0)
    backward(1, 3)
    backward(1, 4)
    dqbuf[1] = (acc[1] * SCALE).astype(BF16)

    @pl.when(has_next)
    def _():
        give_tile(2, 1)
        give_tile(3, 1)

    for a, ref in ((0, dkT), (1, dvT)):
        for half in range(2):
            rows = pl.ds(half * 64, 64)

            @pl.when(has_both)
            def _():
                back(0, a, half).wait_recv()
                snd[2, a, rows] = (ref[2, rows] + rcv[0, a, rows].astype(F32)).astype(BF16)

            @pl.when(last)
            def _():
                snd[2, a, rows] = ref[2, rows].astype(BF16)

            @pl.when(has_prev)
            def _():
                back(2, a, half).start()

    def tail(n, carry):
        backward(0, 3 + n)
        return carry

    lax.fori_loop(0, 2, tail, 0)
    dqbuf[0] = (acc[0] * SCALE).astype(BF16)
    give_tile(2, 0)
    give_tile(3, 0)

    for i in range(2):
        for a, ref in ((0, dkT), (1, dvT)):
            if i == 0:
                @pl.when(has_next)
                def _():
                    returned(1, a)
                    ref[3] = ref[3] + rcv[1, a].astype(F32)

                @pl.when(has_prev)
                def _():
                    returned(3, a)
                    ref[3] = ref[3] + rcv[3, a].astype(F32)
            else:
                @pl.when(has_next)
                def _():
                    returned(2, a)
                    ref[4] = ref[4] + rcv[2, a].astype(F32)

            fin[a, i] = jnp.transpose(ref[3 + i] * (SCALE if a == 0 else 1.0)).astype(BF16)
            give_tile(4 + a, i)

    for a in range(6):
        for dx, c in ALL:
            exchange(a, dx, c).wait_send()
        if a >= 2:
            @pl.when(shift == 1)
            def _():
                exchange(a, 0, core).wait_send()

    def sent(a, part, c):
        for dx in (1, 2, 3):
            give(a, dx, part).wait_send()

        @pl.when(core != c)
        def _():
            give(a, 0, part).wait_send()

    for a in range(6):
        for dx, c in ALL:
            given(a, dx, c).wait_recv()
        if a < 4:
            @pl.when(core == 1)
            def _():
                keep(a, 0).wait()

            @pl.when((core == 0) & has_prev)
            def _():
                given(a, 0, core).wait_recv()

            @pl.when((core == 0) & first)
            def _():
                keep(a, 2).wait()

            sent(a, 0, 1)

            @pl.when(has_next)
            def _():
                for dx in STEPS:
                    give(a, dx, 1).wait_send()

            @pl.when(first)
            def _():
                sent(a, 2, 0)
        else:
            keep(a, core).wait()
            for c in range(2):
                sent(a, c, c)

    @pl.when(has_next)
    def _():
        for a in range(2):
            for dx in STEPS:
                for c in range(2):
                    up(a, dx, c).wait_send()
            for half in range(2):
                back(3, a, half).wait_send()

    @pl.when(has_both)
    def _():
        for a in range(2):
            for dx in STEPS:
                up2(a, dx).wait_send()

    @pl.when(has_prev)
    def _():
        for a in range(2):
            for dx in STEPS:
                down(a, dx).wait_send()
            for half in range(2):
                back(1, a, half).wait_send()
            for half in range(2):
                back(2, a, half).wait_send()

    @pl.when(has_prev2)
    def _():
        for a in range(2):
            for half in range(2):
                back(0, a, half).wait_send()


def write_kernel(*refs):
    sems = refs[-1]
    copies = [pltpu.make_async_copy(refs[i], refs[4 + i], sems.at[i]) for i in range(4)]
    for copy in copies:
        copy.start()
    for copy in copies:
        copy.wait()


def body(pipe, query, key, value, grad_out, segment_ids):
    seg = segment_ids.reshape(-1, D)
    anyspace = pl.BlockSpec(memory_space=pl.ANY)
    dma = pltpu.SemaphoreType.DMA
    hbm = pl.BlockSpec(memory_space=pltpu.HBM)
    shapes = tuple(jax.ShapeDtypeStruct(x.shape, BF16) for x in (query, query, key, value))
    results = pl.pallas_call(
        functools.partial(kernel, pipe),
        out_shape=shapes,
        in_specs=[hbm] * 5,
        out_specs=(anyspace,) * 4,
        scratch_shapes=[
            pltpu.VMEM(seg.shape, jnp.int32),
            pltpu.VMEM((3, 2 * B, D), BF16),
            pltpu.VMEM((3, 2 * B, D), BF16),
            pltpu.VMEM((6 * B, D), BF16),
            pltpu.VMEM((6 * B, D), BF16),
            pltpu.VMEM((3, TILES, B, B), F32),
            pltpu.VMEM((3 * TILES, 2 * B, B), BF16),
            pltpu.VMEM((3 * TILES, 2 * B, D), F32),
            pltpu.VMEM((3, 2 * B, D), F32),
            pltpu.VMEM((3, 2 * B, D), F32),
            pltpu.VMEM((3, 2 * B, D), F32),
            pltpu.VMEM((3, 2 * B, D), F32),
            pltpu.VMEM((3, D, 2 * B), BF16),
            pltpu.VMEM((3, D, 2 * B), BF16),
            pltpu.VMEM((6, D, B), F32),
            pltpu.VMEM((6, D, B), F32),
            pltpu.VMEM((3, 2 * B, D), BF16),
            pltpu.VMEM((3, 2 * B, D), BF16),
            pltpu.VMEM((4, 2, D, B), BF16),
            pltpu.VMEM((4, 2, D, B), BF16),
            pltpu.VMEM((2, 2, B, D), BF16),
            dma(()), dma((6, 4, 3)), dma((6, 4, 3)), dma((6,)),
            dma((64,)), dma((64,)),
            dma((6, 4, 3)), dma((6, 4, 3)), dma((6,)), pltpu.SemaphoreType.REGULAR,
        ],
        compiler_params=pltpu.CompilerParams(
            collective_id=0, has_side_effects=True, vmem_limit_bytes=40 * 1024 * 1024),
    )(*[pltpu.with_memory_space_constraint(x, pltpu.HBM) for x in (query, key, value, grad_out, seg)])
    return pl.pallas_call(
        write_kernel,
        out_shape=shapes,
        in_specs=[pl.BlockSpec(memory_space=pltpu.VMEM)] * 4,
        out_specs=(hbm,) * 4,
        scratch_shapes=[dma((4,))],
    )(*[pltpu.with_memory_space_constraint(x, pltpu.VMEM) for x in results])


def solution(mesh):
    spec = P(("pipe", "tensor"), None)
    return jax.shard_map(
        functools.partial(body, mesh.shape["pipe"]),
        mesh=mesh,
        in_specs=(spec,) * 4 + (P(),),
        out_specs=(spec,) * 4,
        check_vma=False,
    )
```
